512 devices in a mesh: grp: 4 (over x), dev: 128 (over z, y, core).
Axes of the slice: x: 4, y: 4, z: 16, core: 2. Of those that a mesh axis runs over, the one named last changes fastest.
Arguments:
- leaf_emit: float32 [3, 65536], P(None, 'dev'), may hold values from 0 to 1
- leaf_albedo: float32 [3, 65536], P(None, 'dev'), may hold values from 0.2 to 0.9
- leaf_radiosity: float32 [3, 65536], P(None, 'dev'), may hold values from 0.05 to 4
- leaf_area: float32 [65536], P('dev'), may hold values from 0.002 to 0.03
- parent_index: int32 [65536], P('dev'), may hold values from 0 to 255, as said below
- node_position: float32 [3, 98304], P(None, 'dev'), may hold values from -1 to 1
- node_angles: float32 [2, 98304], P(None, 'dev'), may hold values from -3.140625 to 3.140625
- block_receiver: int32 [4, 16384], P('grp', 'dev'), may hold values from 0 to 5
- block_source: int32 [4, 16384], P('grp', 'dev'), may hold values from 0 to 255
- block_count: int32 [4, 128], P('grp', 'dev'), may hold values from 16 to 128, as said below
Outputs:
- new_radiosity: float32 [3, 65536], P(None, 'dev')
The draws below stay inside these ranges and needn't reach their ends.
Inputs may be any that keep to these rules, and one draw needn't show every extreme that they name: `parent_index`: within each shard's 512 leaves every cluster 0 to 255 is named at least once. The first block_count slots of a device are live, the rest are ignored. For every index of dev exactly one index of grp has 128 live slots; the others have at most 64.
All inputs are finite; a program needn't handle non-finite values.
Results may differ from the reference program's by a relative error of at most 0.0001.
Values sent between devices are 32-bit elements; how exact they have to be, the bound alone decides.
No kernel may reach another device: no remote copies, remote signals or barrier semaphores. Data moves between devices by JAX's collectives and lax.ppermute only.
A program may use at most 64 MiB of HBM per device.

```python
import math
import jax
import jax.numpy as jnp
from jax import lax

TILE = 128
LEAF_DEV = 512
PAR_DEV = 256
BLK = 128
GROUPS = 4
SHARDS = 128
NODE_DEV = 768
NT = 6
SRC_TILES = 256
LEAVES = 65536
NODES = 98304


def draw_parent_index(key, part):
    shard_count = LEAVES // LEAF_DEV
    shard_keys = jax.random.split(key, shard_count)

    def one_shard(shard_key):
        first_key, second_key = jax.random.split(shard_key)
        covered = jnp.arange(PAR_DEV, dtype=jnp.int32)
        others = jax.random.randint(first_key, (LEAF_DEV - PAR_DEV,), 0, PAR_DEV, dtype=jnp.int32)
        return jax.random.permutation(second_key, jnp.concatenate([covered, others]))
    return jax.vmap(one_shard)(shard_keys).reshape(LEAVES).astype(jnp.int32)


def draw_block_count(key, part):
    first_key, second_key = jax.random.split(jax.random.fold_in(key, 7))
    counts = jax.random.randint(first_key, (GROUPS, SHARDS), BLK // 8, BLK // 2 + 1, dtype=jnp.int32)
    heavy = jax.random.randint(second_key, (SHARDS,), 0, GROUPS, dtype=jnp.int32)
    group_rows = jnp.arange(GROUPS, dtype=jnp.int32)[:, None]
    return jnp.where(group_rows == heavy[None, :], BLK, counts).astype(jnp.int32)


def set_ends(entries, rng, least, high):
    longest = entries.shape.index(max(entries.shape))
    spots = []
    for shift in (0, 1):
        where = [jax.random.randint(jax.random.fold_in(rng, axis), (), 0, length) for axis, length in enumerate(entries.shape)]
        where[longest] = (where[longest] + shift) % entries.shape[longest]
        spots.append(tuple(where))
    return entries.at[spots[0]].set(least).at[spots[1]].set(high)


def steps_of(stream_key, extent, pieces, low, high):
    factor_of, own = 1.0, jax.random.fold_in(stream_key, 6)
    for position, shards_of in pieces:
        draws = jnp.exp(jax.random.uniform(jax.random.fold_in(own, position), (shards_of,), jnp.float32, low / len(pieces), high / len(pieces)))
        factor_of = factor_of * jnp.repeat(draws, extent[position] // shards_of).reshape([-1 if axis == position else 1 for axis in range(len(extent))])
    return factor_of


def setup_inputs(seed: int = 0) -> dict:
    key_list = jax.random.split(jax.random.key(seed), 11)
    leaf_emit = jnp.clip(1.0 * jax.random.uniform(key_list[0], (3, LEAVES), jnp.float32) ** steps_of(key_list[0], (3, LEAVES), ((1, 128),), -0.2, 0.2), 0.0, 1.0)
    leaf_albedo = jnp.clip(0.2 + 0.7 * jax.random.uniform(key_list[1], (3, LEAVES), jnp.float32) ** steps_of(key_list[1], (3, LEAVES), ((1, 128),), -0.2, 0.2), 0.2, 0.9)
    leaf_radiosity = jnp.clip(jnp.exp(math.log(4.0) - 4.3820266 * jax.random.uniform(key_list[2], (3, LEAVES), jnp.float32) ** steps_of(key_list[2], (3, LEAVES), ((1, 128),), -0.2, 0.2)), 0.05, 4.0)
    leaf_area = jnp.clip(jnp.exp(math.log(0.03) - 2.70805 * jax.random.uniform(key_list[3], (LEAVES,), jnp.float32) ** steps_of(key_list[3], (LEAVES,), ((0, 128),), -0.2, 0.2)), 0.002, 0.03)
    parent_index = draw_parent_index(jax.random.fold_in(key_list[10], 71), 0)
    node_position = jnp.clip(jax.random.uniform(key_list[5], (3, NODES), jnp.float32, -1.0, 1.0) * steps_of(key_list[5], (3, NODES), ((1, 128),), -0.4, 0.0), -1.0, 1.0)
    node_angles = jnp.clip(jax.random.uniform(key_list[6], (2, NODES), jnp.float32, -3.140625, 3.140625), -3.140625, 3.140625)
    block_receiver = set_ends(jax.random.randint(key_list[7], (GROUPS, SHARDS * BLK), 0, NT), jax.random.fold_in(key_list[7], 1), 0, NT - 1).astype(jnp.int32)
    block_source = set_ends(jax.random.randint(key_list[8], (GROUPS, SHARDS * BLK), 0, SRC_TILES), jax.random.fold_in(key_list[8], 1), 0, SRC_TILES - 1).astype(jnp.int32)
    block_count = draw_block_count(jax.random.fold_in(key_list[10], 71), 0)
    return {"leaf_emit": leaf_emit, "leaf_albedo": leaf_albedo, "leaf_radiosity": leaf_radiosity, "leaf_area": leaf_area, "parent_index": parent_index, "node_position": node_position, "node_angles": node_angles, "block_receiver": block_receiver, "block_source": block_source, "block_count": block_count}


def unit_normals(node_angles):
    azimuth = node_angles[0]
    elevation = node_angles[1]
    return jnp.stack([jnp.cos(azimuth) * jnp.cos(elevation), jnp.sin(azimuth) * jnp.cos(elevation), jnp.sin(elevation)])


def tile_irradiance(receivers, sources):
    offsets = [sources[axis_id][:, None, :] - receivers[axis_id][:, :, None] for axis_id in range(3)]
    distance_sq = offsets[0] * offsets[0] + offsets[1] * offsets[1] + offsets[2] * offsets[2]
    facing_receiver = receivers[3][:, :, None] * offsets[0] + receivers[4][:, :, None] * offsets[1] + receivers[5][:, :, None] * offsets[2]
    facing_source = sources[3][:, None, :] * offsets[0] + sources[4][:, None, :] * offsets[1] + sources[5][:, None, :] * offsets[2]
    source_area = sources[6][:, None, :]
    factor = source_area * jnp.maximum(facing_receiver, 0.0) * jnp.maximum(-facing_source, 0.0) / ((distance_sq + source_area) * (jnp.pi * distance_sq + source_area))
    return jnp.einsum('bij,cbj->bci', factor, sources[7:10], precision=lax.Precision.HIGHEST)


def reference(leaf_emit, leaf_albedo, leaf_radiosity, leaf_area, parent_index, node_position, node_angles, block_receiver, block_source, block_count):
    shard_count = SHARDS
    per_peer = NODE_DEV // shard_count
    normals = unit_normals(node_angles)
    positions = node_position.reshape(3, shard_count, NODE_DEV)
    normals = normals.reshape(3, shard_count, NODE_DEV)
    patch_area = leaf_area.reshape(shard_count, LEAF_DEV)
    radiosity = leaf_radiosity.reshape(3, shard_count, LEAF_DEV)
    parents = parent_index.reshape(shard_count, LEAF_DEV)
    parent_onehot = (parents[:, :, None] == jnp.arange(PAR_DEV, dtype=jnp.int32)[None, None, :]).astype(jnp.float32)
    cluster_area = jnp.einsum('sl,slp->sp', patch_area, parent_onehot, precision=lax.Precision.HIGHEST)
    weighted = jnp.einsum('csl,slp->csp', radiosity * patch_area[None], parent_onehot, precision=lax.Precision.HIGHEST)
    cluster_radiosity = weighted / cluster_area[None]
    source_pack = jnp.concatenate([positions[:, :, LEAF_DEV:], normals[:, :, LEAF_DEV:], cluster_area[None], cluster_radiosity], axis=0)
    source_tiles = source_pack.reshape(10, SRC_TILES, TILE)
    receiver_octree = jnp.concatenate([positions, normals], axis=0)
    receiver_link = receiver_octree.reshape(6, shard_count, shard_count, per_peer).transpose(0, 2, 1, 3)
    receiver_tiles = receiver_link.reshape(6, shard_count * NT, TILE)
    tile_offset = (jnp.arange(shard_count, dtype=jnp.int32) * NT)[None, :, None]
    receiver_ids = (block_receiver.reshape(GROUPS, shard_count, BLK) + tile_offset).reshape(GROUPS * shard_count, BLK)
    source_ids = block_source.reshape(GROUPS * shard_count, BLK)
    live_weight = (jnp.arange(BLK, dtype=jnp.int32)[None, None, :] < block_count[:, :, None]).astype(jnp.float32)
    live_weight = live_weight.reshape(GROUPS * shard_count, BLK)

    def accumulate(totals, batch):
        batch_receivers, batch_sources, batch_weight = batch
        receivers = jnp.take(receiver_tiles, batch_receivers, axis=1)
        sources = jnp.take(source_tiles, batch_sources, axis=1)
        contrib = tile_irradiance(receivers, sources) * batch_weight[:, None, None]
        return totals.at[batch_receivers].add(contrib), None

    initial = jnp.zeros((shard_count * NT, 3, TILE), jnp.float32)
    totals, unused = lax.scan(accumulate, initial, (receiver_ids, source_ids, live_weight))
    link_order = totals.reshape(shard_count, NT, 3, TILE).transpose(2, 0, 1, 3).reshape(3, shard_count, NODE_DEV)
    octree_order = link_order.reshape(3, shard_count, shard_count, per_peer).transpose(0, 2, 1, 3).reshape(3, shard_count, NODE_DEV)
    pushed = jnp.einsum('csp,slp->csl', octree_order[:, :, LEAF_DEV:], parent_onehot, precision=lax.Precision.HIGHEST)
    gathered = octree_order[:, :, :LEAF_DEV] + pushed
    return leaf_emit + leaf_albedo * gathered.reshape(3, shard_count * LEAF_DEV)
```

```python
import functools
import math

import jax
import jax.numpy as jnp
from jax import lax
from jax.experimental import pallas as pl
from jax.experimental.pallas import tpu as pltpu
from jax.sharding import Mesh
from jax.sharding import PartitionSpec as P

TILE = 128
DEV = ("dev_0", "dev_1", "dev_2")
QUAD = 4
PACK = 20
FIELDS = 9
OFFSETS = 248
EMPTY = 40
EXACT = lax.Precision.HIGHEST
NT_DIMS = (((1,), (1,)), ((), ()))


def pack_kernel(
    radiosity, area, parent, position, angles, receiver, source, count, pack_out, nodes_out
):
    leaf_count = area.shape[1]
    node_count = position.shape[1]
    cluster_count = node_count - leaf_count
    azimuth = angles[0:1, :]
    elevation = angles[1:2, :]
    cos_e = jnp.cos(elevation)
    nodes_out[0:3, :] = position[...]
    nodes_out[3:4, :] = jnp.cos(azimuth) * cos_e
    nodes_out[4:5, :] = jnp.sin(azimuth) * cos_e
    nodes_out[5:6, :] = jnp.sin(elevation)
    nodes_out[6:8, :] = jnp.zeros((2, node_count), jnp.float32)
    clusters = lax.broadcasted_iota(jnp.int32, (cluster_count, leaf_count), 0)
    onehot = (clusters == parent[...]).astype(jnp.float32)
    leaf_area = area[...]
    values = jnp.concatenate(
        [leaf_area, radiosity[...] * leaf_area, jnp.zeros((4, leaf_count), jnp.float32)], axis=0
    )
    sums = lax.dot_general(
        values, onehot, NT_DIMS, precision=EXACT, preferred_element_type=jnp.float32
    )
    cluster_area = sums[0:1, :]
    cluster_radiosity = sums[1:4, :] / cluster_area
    scaled = nodes_out[3:6, leaf_count:] * (cluster_area * (-1.0 / math.pi))
    slots = receiver.shape[1]
    tiles = lax.broadcasted_iota(jnp.int32, (8, slots), 0)
    lanes = lax.broadcasted_iota(jnp.int32, (8, slots), 1)
    live = lanes < count[...]
    member = jnp.where((tiles == receiver[...]) & live, 1.0, 0.0)
    before = (
        lax.broadcasted_iota(jnp.int32, (slots, slots), 0)
        < lax.broadcasted_iota(jnp.int32, (slots, slots), 1)
    ).astype(jnp.float32)
    place = jnp.dot(member, before, preferred_element_type=jnp.float32)
    held = jnp.sum(member, axis=1, keepdims=True)
    quads = jnp.broadcast_to(jnp.floor((held + (QUAD - 1)) * (1.0 / QUAD)), (8, slots))
    first = jnp.zeros((8, slots), jnp.float32)
    for t in range(7):
        first = first + jnp.where(tiles > t, quads[t : t + 1, :], 0.0)
    spot = jnp.sum(member * (first * QUAD + place), axis=0, keepdims=True)
    alive = jnp.sum(member, axis=0, keepdims=True)
    spot = jnp.where(alive > 0.0, spot, -1.0).astype(jnp.int32)
    to_spot = (lax.broadcasted_iota(jnp.int32, (2 * slots, slots), 0) == spot).astype(jnp.float32)
    entries = jnp.broadcast_to((source[...] + 1).astype(jnp.float32), (8, slots))
    ordered = lax.dot_general(entries, to_spot, NT_DIMS, preferred_element_type=jnp.float32)
    offsets = jnp.sum(
        jnp.where(lanes == OFFSETS - TILE + tiles, first, 0.0), axis=0, keepdims=True
    )
    rows = []
    for half in range(2):
        cols = slice(half * TILE, half * TILE + TILE)
        at = slice(leaf_count + half * TILE, leaf_count + half * TILE + TILE)
        rows += [position[:, at], scaled[:, cols], cluster_radiosity[:, cols]]
    rows += [ordered[0:1, :TILE], ordered[0:1, TILE:] + offsets]
    packed = jnp.concatenate(rows, axis=0)
    for peer in range(pack_out.shape[0]):
        pack_out[peer] = packed


def gather_kernel(
    where_ref,
    sources_hbm,
    nodes_ref,
    parent_ref,
    out_ref,
    sources,
    area,
    area_pi,
    receivers,
    totals,
    table_vmem,
    table,
    sem,
    table_sem,
    *,
    sizes,
):
    shard_z, shard_y, shard_c = sizes
    shards = shard_z * shard_y * shard_c
    node_count = nodes_ref.shape[1]
    per_peer = node_count // shards
    null_row = shards * PACK
    copy = pltpu.make_async_copy(sources_hbm, sources.at[pl.ds(0, null_row)], sem)
    copy.start()
    for chunk in range(node_count // TILE):
        at = slice(chunk * TILE, chunk * TILE + TILE)
        turned = nodes_ref[:, at].T
        for field in range(6):
            receivers[field, at, :] = jnp.broadcast_to(turned[:, field : field + 1], (TILE, TILE))
    for field in range(6):
        receivers[field, node_count : node_count + 8, :] = jnp.zeros((8, TILE), jnp.float32)
    copy.wait()
    sources[null_row : null_row + 16, :] = jnp.zeros((16, TILE), jnp.float32)
    area[null_row : null_row + 8, :] = jnp.ones((8, TILE), jnp.float32)
    area_pi[null_row : null_row + 8, :] = jnp.ones((8, TILE), jnp.float32)
    for half in range(2):
        base = half * FIELDS
        bx, by, bz = (sources[pl.ds(base + 3 + a, shards, stride=PACK), :] for a in range(3))
        length = jnp.sqrt(bx * bx + by * by + bz * bz)
        area_pi[pl.ds(base, shards, stride=PACK), :] = length
        area[pl.ds(base, shards, stride=PACK), :] = length * math.pi
    column = lax.broadcasted_iota(jnp.int32, (shard_z, TILE), 1)
    per_c = shard_y * shard_z

    def source_row(entry):
        tile = entry - 1
        half = tile & 1
        owner = tile >> 1
        arrival = (
            (owner & (shard_c - 1)) * per_c
            + ((owner // shard_c) & (shard_y - 1)) * shard_z
            + owner // (shard_c * shard_y)
        )
        return jnp.where(entry == 0, null_row, arrival * PACK + half * FIELDS)

    for c in range(shard_c):
        for y in range(shard_y):
            begin = (c * per_c + y * shard_z) * PACK + 2 * FIELDS
            low = sources[pl.ds(begin, shard_z, stride=PACK), :].astype(jnp.int32)
            high = sources[pl.ds(begin + 1, shard_z, stride=PACK), :].astype(jnp.int32)
            rows = pl.ds(y * shard_c + c, shard_z, stride=shard_y * shard_c)
            table_vmem[0, rows, :] = source_row(low)
            table_vmem[1, rows, :] = jnp.where(column < OFFSETS - TILE, source_row(high), high)
    extra = lax.broadcasted_iota(jnp.int32, (8, TILE), 1)
    table_vmem[0, shards : shards + 8, :] = jnp.full((8, TILE), null_row, jnp.int32)
    table_vmem[1, shards : shards + 8, :] = jnp.where(extra < OFFSETS - TILE, null_row, 0)
    to_smem = pltpu.make_async_copy(table_vmem, table, table_sem)
    to_smem.start()
    to_smem.wait()

    first_tile = where_ref[0] * per_peer // TILE
    last_tile = (where_ref[0] * per_peer + per_peer - 1) // TILE

    def run_pass(which, tile):
        def enter(shard):
            begin = table[1, shard, OFFSETS - TILE + tile]
            end = table[1, shard, OFFSETS - TILE + tile + 1]
            empty = begin == end
            return jnp.where(empty, EMPTY, begin), jnp.where(empty, EMPTY + 1, end)

        def one_quad(state):
            shard, quad, end, keep, acc = state
            node = shard * per_peer
            rec = [receivers[field, pl.ds(node, 8), :] for field in range(6)]
            acc = [a * keep for a in acc]
            plane = (quad * QUAD) // TILE
            spot = (quad * QUAD) % TILE
            for u in range(QUAD):
                row = table[plane, shard, spot + u]
                src = [sources[pl.ds(row + f, 1), :] for f in range(FIELDS)]
                d = [src[a] - rec[a] for a in range(3)]
                r2 = d[0] * d[0] + d[1] * d[1] + d[2] * d[2]
                toward = rec[3] * d[0] + rec[4] * d[1] + rec[5] * d[2]
                back = src[3] * d[0] + src[4] * d[1] + src[5] * d[2]
                top = jnp.maximum(toward, 0.0) * jnp.maximum(back, 0.0)
                bottom = (r2 + area[pl.ds(row, 1), :]) * (r2 + area_pi[pl.ds(row, 1), :])
                factor = top / bottom
                acc = [acc[c] + factor * src[6 + c] for c in range(3)]
            for c in range(3):
                totals[which, c, pl.ds(node, 8), :] = acc[c]
            quad = quad + 1
            done = quad >= end
            shard = jnp.where(done, shard + 1, shard)
            begin_next, end_next = enter(shard)
            quad = jnp.where(done, begin_next, quad)
            end = jnp.where(done, end_next, end)
            keep = jnp.where(done, 0.0, 1.0)
            return shard, quad, end, keep, acc

        def step(state):
            for _ in range(2):
                state = one_quad(state)
            return state

        begin, end = enter(0)
        zero = jnp.zeros((8, TILE), jnp.float32)
        lax.while_loop(
            lambda state: state[0] < shards,
            step,
            (jnp.int32(0), begin, end, jnp.float32(0.0), [zero, zero, zero]),
        )

    run_pass(0, first_tile)
    straddles = last_tile > first_tile

    @pl.when(straddles)
    def _():
        run_pass(1, last_tile)
        split = last_tile * TILE - where_ref[0] * per_peer
        within = lax.broadcasted_iota(jnp.int32, (node_count, TILE), 0) % per_peer
        for c in range(3):
            totals[0, c, 0:node_count, :] = jnp.where(
                within >= split, totals[1, c, 0:node_count, :], totals[0, c, 0:node_count, :]
            )

    ones = jnp.ones((8, TILE), jnp.float32)
    irradiance = jnp.concatenate(
        [
            lax.dot_general(
                ones,
                totals[0, c, 0:node_count, :],
                NT_DIMS,
                precision=EXACT,
                preferred_element_type=jnp.float32,
            )[0:1, :]
            for c in range(3)
        ]
        + [jnp.zeros((5, node_count), jnp.float32)],
        axis=0,
    )
    leaf_count = parent_ref.shape[1]
    cluster_count = node_count - leaf_count
    clusters = lax.broadcasted_iota(jnp.int32, (cluster_count, leaf_count), 0)
    onehot = (clusters == parent_ref[...]).astype(jnp.float32)
    pushed = jnp.dot(
        irradiance[:, leaf_count:], onehot, precision=EXACT, preferred_element_type=jnp.float32
    )
    gathered = (irradiance[:, :leaf_count] + pushed)[0:3, :]
    for group in range(out_ref.shape[0]):
        out_ref[group] = gathered


def body(
    leaf_emit,
    leaf_albedo,
    leaf_radiosity,
    leaf_area,
    parent_index,
    node_position,
    node_angles,
    block_receiver,
    block_source,
    block_count,
):
    leaf_count = leaf_area.shape[0]
    node_count = node_position.shape[1]
    sizes = tuple(lax.axis_size(axis) for axis in DEV)
    shards = sizes[0] * sizes[1] * sizes[2]
    groups = lax.axis_size("grp")
    parent = parent_index[None, :]
    vmem = pl.BlockSpec(memory_space=pltpu.VMEM)
    pack, nodes = pl.pallas_call(
        pack_kernel,
        out_shape=(
            jax.ShapeDtypeStruct((sizes[0], PACK, TILE), jnp.float32),
            jax.ShapeDtypeStruct((8, node_count), jnp.float32),
        ),
        in_specs=[vmem] * 8,
        out_specs=(vmem, vmem),
        name="pack",
    )(
        leaf_radiosity,
        leaf_area[None, :],
        parent,
        node_position,
        node_angles,
        block_receiver,
        block_source,
        block_count,
    )
    held = pack.reshape(sizes[0], PACK // 4, 4, TILE)
    held = lax.all_to_all(held, DEV[0], 0, 0, tiled=True)
    for axis, size in zip(DEV[1:], sizes[1:]):
        held = held.reshape(-1, 4, TILE)
        held = lax.all_to_all(
            jnp.broadcast_to(held[None], (size, *held.shape)), axis, 0, 0, tiled=True
        )
    everything = held.reshape(shards * PACK, TILE)
    where = lax.axis_index(DEV).astype(jnp.int32).reshape(1)
    rows = shards * PACK
    partial = pl.pallas_call(
        functools.partial(gather_kernel, sizes=sizes),
        out_shape=jax.ShapeDtypeStruct((groups, 3, leaf_count), jnp.float32),
        in_specs=[
            pl.BlockSpec(memory_space=pltpu.SMEM),
            pl.BlockSpec(memory_space=pl.ANY),
            vmem,
            vmem,
        ],
        out_specs=vmem,
        scratch_shapes=[
            pltpu.VMEM((rows + 16, TILE), jnp.float32),
            pltpu.VMEM((rows + 16, TILE), jnp.float32),
            pltpu.VMEM((rows + 16, TILE), jnp.float32),
            pltpu.VMEM((6, node_count + 8, TILE), jnp.float32),
            pltpu.VMEM((2, 3, node_count + 8, TILE), jnp.float32),
            pltpu.VMEM((2, shards + 8, TILE), jnp.int32),
            pltpu.SMEM((2, shards + 8, TILE), jnp.int32),
            pltpu.SemaphoreType.DMA(()),
            pltpu.SemaphoreType.DMA(()),
        ],
        compiler_params=pltpu.CompilerParams(vmem_limit_bytes=40 * 1024 * 1024),
        name="gather",
    )(where, everything, nodes, parent)
    gathered = lax.all_to_all(partial, "grp", 0, 0, tiled=True).sum(axis=0)
    return leaf_emit + leaf_albedo * gathered


def solution(mesh):
    split = Mesh(
        mesh.devices.reshape(mesh.shape["grp"], 16, 4, 2), ("grp", "dev_0", "dev_1", "dev_2")
    )
    placed = (
        P(None, DEV),
        P(None, DEV),
        P(None, DEV),
        P(DEV),
        P(DEV),
        P(None, DEV),
        P(None, DEV),
        P("grp", DEV),
        P("grp", DEV),
        P("grp", DEV),
    )
    return jax.shard_map(body, mesh=split, in_specs=placed, out_specs=P(None, DEV), check_vma=False)
```

```python
import functools
import math

import jax
import jax.numpy as jnp
from jax import lax
from jax.experimental import pallas as pl
from jax.experimental.pallas import tpu as pltpu
from jax.sharding import Mesh
from jax.sharding import PartitionSpec as P

TILE = 128
DEV = ("dev_0", "dev_1", "dev_2")
QUAD = 4
STEP = 4
PACK = 20
FIELDS = 9
SOURCE = 16
OFFSETS = 248
EMPTY = 40
START = 254
STOP = 255
HEAD = 32
EXACT = lax.Precision.HIGHEST
NT_DIMS = (((1,), (1,)), ((), ()))


def lane_rows(array):
    return [array[:, at : at + TILE] for at in range(0, array.shape[1], TILE)]


def pack_kernel(
    radiosity, area, parent, position, angles, receiver, source, count, pack_out, local_out
):
    leaf_count = area.shape[1]
    node_count = position.shape[1]
    cluster_count = node_count - leaf_count
    azimuth = angles[0:1, :]
    elevation = angles[1:2, :]
    cos_e = jnp.cos(elevation)
    nodes = [position[a : a + 1, :] for a in range(3)]
    nodes += [jnp.cos(azimuth) * cos_e, jnp.sin(azimuth) * cos_e, jnp.sin(elevation)]
    clusters = lax.broadcasted_iota(jnp.int32, (cluster_count, leaf_count), 0)
    onehot = (clusters == parent[...]).astype(jnp.float32)
    leaf_area = area[...]
    values = jnp.concatenate(
        [leaf_area, radiosity[...] * leaf_area, jnp.zeros((4, leaf_count), jnp.float32)], axis=0
    )
    sums = lax.dot_general(
        values, onehot, NT_DIMS, precision=EXACT, preferred_element_type=jnp.float32
    )
    cluster_area = sums[0:1, :]
    cluster_radiosity = sums[1:4, :] / cluster_area
    scale = cluster_area * (-1.0 / math.pi)
    slots = receiver.shape[1]
    tiles = lax.broadcasted_iota(jnp.int32, (8, slots), 0)
    lanes = lax.broadcasted_iota(jnp.int32, (8, slots), 1)
    live = lanes < count[...]
    member = jnp.where((tiles == receiver[...]) & live, 1.0, 0.0)
    before = (
        lax.broadcasted_iota(jnp.int32, (slots, slots), 0)
        < lax.broadcasted_iota(jnp.int32, (slots, slots), 1)
    ).astype(jnp.float32)
    place = jnp.dot(member, before, preferred_element_type=jnp.float32)
    held = jnp.sum(member, axis=1, keepdims=True)
    quads = jnp.broadcast_to(jnp.floor((held + (QUAD - 1)) * (1.0 / QUAD)), (8, slots))
    first = jnp.zeros((8, slots), jnp.float32)
    for t in range(7):
        first = first + jnp.where(tiles > t, quads[t : t + 1, :], 0.0)
    spot = jnp.sum(member * (first * QUAD + place), axis=0, keepdims=True)
    alive = jnp.sum(member, axis=0, keepdims=True)
    spot = jnp.where(alive > 0.0, spot, -1.0).astype(jnp.int32)
    to_spot = (lax.broadcasted_iota(jnp.int32, (2 * slots, slots), 0) == spot).astype(jnp.float32)
    entries = jnp.broadcast_to((source[...] + 1).astype(jnp.float32), (8, slots))
    ordered = lax.dot_general(entries, to_spot, NT_DIMS, preferred_element_type=jnp.float32)
    offsets = jnp.sum(
        jnp.where(lanes == OFFSETS - TILE + tiles, first, 0.0), axis=0, keepdims=True
    )
    rows = []
    for half in range(cluster_count // TILE):
        cols = slice(half * TILE, half * TILE + TILE)
        at = slice(leaf_count + half * TILE, leaf_count + half * TILE + TILE)
        rows += [nodes[a][:, at] for a in range(3)]
        rows += [nodes[a][:, at] * scale[:, cols] for a in range(3, 6)]
        rows += [cluster_radiosity[c : c + 1, cols] for c in range(3)]
    rows += [ordered[0:1, :TILE], ordered[0:1, TILE:] + offsets]
    for piece in range(PACK // 4):
        part = jnp.concatenate(rows[piece * 4 : piece * 4 + 4], axis=0)
        for peer in range(pack_out.shape[0]):
            pack_out[peer, piece] = part
    local = [row for field in nodes for row in lane_rows(field)]
    local += lane_rows(parent[...].astype(jnp.float32))
    local += [jnp.zeros((1, TILE), jnp.float32)] * (local_out.shape[0] * 4 - len(local))
    for piece in range(len(local) // 4):
        local_out[piece] = jnp.concatenate(local[piece * 4 : piece * 4 + 4], axis=0)


def gather_kernel(
    where_ref,
    held_ref,
    out_ref,
    sources,
    dense,
    receivers,
    totals,
    table_vmem,
    table,
    sems,
    *,
    sizes,
    node_count,
    leaf_count,
):
    shard_z, shard_y, shard_c = sizes
    shards = shard_z * shard_y * shard_c
    tiles = 2 * shards
    per_c = shard_y * shard_z
    per_peer = node_count // shards
    chunks = node_count // TILE
    block = held_ref.shape[0] // shard_c
    local = per_c * PACK
    here = where_ref[0]
    core = here & (shard_c - 1)

    def tile_of(shard):
        low = shard * per_peer // TILE
        high = (shard * per_peer + per_peer - 1) // TILE
        split = jnp.where(high > low, high * TILE - shard * per_peer, per_peer)
        late = split * 2 < per_peer
        return jnp.where(late, high, low), split, late

    tile, split, late = tile_of(here)
    partner = here ^ 1
    _, partner_split, partner_late = tile_of(partner)
    helps = partner_split < per_peer
    helped = jnp.where(partner_late, 0, partner_split)
    helped_count = jnp.where(partner_late, partner_split, per_peer - partner_split)

    column = lax.broadcasted_iota(jnp.int32, (shard_z, TILE), 1)
    beyond = tiles * SOURCE

    def source_tile(entry):
        tile = entry - 1
        owner = tile >> 1
        arrival = (
            (owner & (shard_c - 1)) * per_c
            + ((owner >> (shard_c.bit_length() - 1)) & (shard_y - 1)) * shard_z
            + (owner >> ((shard_c * shard_y).bit_length() - 1))
        )
        return jnp.where(entry == 0, beyond, (arrival * 2 + (tile & 1)) * SOURCE)

    def read(rows, at):
        return jnp.sum(jnp.where(column == at, rows, 0), axis=1, keepdims=True) * QUAD

    for c in range(shard_c):
        for y in range(shard_y):
            begin = c * block + y * shard_z * PACK + 2 * FIELDS
            low = held_ref[pl.ds(begin, shard_z, stride=PACK), :].astype(jnp.int32)
            high = held_ref[pl.ds(begin + 1, shard_z, stride=PACK), :].astype(jnp.int32)
            start = read(high, OFFSETS - TILE + tile)
            stop = read(high, OFFSETS - TILE + tile + 1)
            empty = start == stop
            start = jnp.where(empty, EMPTY * QUAD, start)
            stop = jnp.where(empty, EMPTY * QUAD + QUAD, stop)
            rest = jnp.where(column < OFFSETS - TILE, source_tile(high), 0)
            rest = jnp.where(column == START - TILE, start, rest)
            rest = jnp.where(column == STOP - TILE, stop, rest)
            rows = pl.ds(y * shard_c + c, shard_z, stride=shard_y * shard_c)
            table_vmem[0, rows, :] = source_tile(low)
            table_vmem[1, rows, :] = rest
    extra = lax.broadcasted_iota(jnp.int32, (8, TILE), 1)
    table_vmem[0, shards : shards + 8, :] = jnp.full((8, TILE), beyond, jnp.int32)
    last = jnp.where(extra == START - TILE, EMPTY * QUAD, beyond)
    last = jnp.where(extra == STOP - TILE, EMPTY * QUAD + QUAD, last)
    table_vmem[1, shards : shards + 8, :] = last
    fetches = [
        pltpu.make_async_copy(
            table_vmem.at[half, pl.ds(at, size), :],
            table.at[pl.ds(at, size), pl.ds(half * TILE, TILE)],
            sems.at[n, half],
        )
        for n, (at, size) in enumerate(((0, HEAD), (HEAD, shards + 8 - HEAD)))
        for half in range(2)
    ]
    for fetch in fetches:
        fetch.start()

    for c in range(shard_c):
        for half in range(2):
            base = c * block + half * FIELDS
            rows = [held_ref[pl.ds(base + f, per_c, stride=PACK), :] for f in range(FIELDS)]
            length = jnp.sqrt(rows[3] * rows[3] + rows[4] * rows[4] + rows[5] * rows[5])
            rows += [length * math.pi, length]
            for f, row in enumerate(rows):
                at = c * per_c * 2 * SOURCE + half * SOURCE + f
                sources[pl.ds(at, per_c, stride=2 * SOURCE), :] = row
    blank = lax.broadcasted_iota(jnp.int32, (SOURCE, TILE), 0) >= FIELDS
    sources[tiles * SOURCE : (tiles + 1) * SOURCE, :] = blank.astype(jnp.float32)

    def spread(owner):
        for chunk in range(chunks):
            turned = held_ref[pl.ds(owner * block + local + chunk, 8, stride=chunks), :].T
            for field in range(6):
                dense[field, 8 + chunk * TILE : 8 + (chunk + 1) * TILE, :] = jnp.broadcast_to(
                    turned[:, field : field + 1], (TILE, TILE)
                )

    for field in range(6):
        dense[field, 0:8, :] = jnp.zeros((8, TILE), jnp.float32)
        dense[field, 8 + node_count : 16 + node_count, :] = jnp.zeros((8, TILE), jnp.float32)
        receivers[field, shards * 8 : (shards + 8) * 8, :] = jnp.zeros((64, TILE), jnp.float32)
    spread(core)

    def settle(link, carry):
        for field in range(6):
            receivers[field, pl.ds(pl.multiple_of(link * 8, 8), 8), :] = dense[
                field, pl.ds(8 + link * per_peer, 8), :
            ]
        return carry

    lax.fori_loop(0, shards, settle, 0, unroll=8)

    @pl.when(helps)
    def _():
        spread(1 - core)
        keep = lax.broadcasted_iota(jnp.int32, (8, TILE), 0) < per_peer

        def join(link, carry):
            for field in range(6):
                rows = pl.ds(pl.multiple_of(link * 8, 8), 8)
                theirs = dense[field, pl.ds(8 + link * per_peer + helped - per_peer, 8), :]
                receivers[field, rows, :] = jnp.where(keep, receivers[field, rows, :], theirs)
            return carry

        lax.fori_loop(0, shards, join, 0, unroll=4)

    def one_quad(state):
        shard, spot, end, keep, acc = state
        at = pl.ds(pl.multiple_of(shard * 8, 8), 8)
        rec = [receivers[field, at, :] for field in range(6)]
        acc = [a * keep for a in acc]
        for u in range(QUAD):
            row = pl.multiple_of(table[shard, spot + u], SOURCE)
            src = [sources[pl.ds(row + f, 1), :] for f in range(FIELDS + 2)]
            d = [src[a] - rec[a] for a in range(3)]
            r2 = d[0] * d[0] + d[1] * d[1] + d[2] * d[2]
            toward = rec[3] * d[0] + rec[4] * d[1] + rec[5] * d[2]
            back = src[3] * d[0] + src[4] * d[1] + src[5] * d[2]
            top = jnp.maximum(toward, 0.0) * jnp.maximum(back, 0.0)
            factor = top / ((r2 + src[9]) * (r2 + src[10]))
            acc = [acc[c] + factor * src[6 + c] for c in range(3)]
        for c in range(3):
            totals[c, at, :] = acc[c]
        spot = spot + QUAD
        done = spot >= end
        spot = jnp.where(done, table[shard + 1, START], spot)
        end = jnp.where(done, table[shard + 1, STOP], end)
        shard = jnp.where(done, shard + 1, shard)
        keep = jnp.where(done, 0.0, 1.0)
        return shard, spot, end, keep, acc

    def step(state):
        for _ in range(STEP):
            state = one_quad(state)
        return state

    for fetch in fetches[:2]:
        fetch.wait()
    zero = jnp.zeros((8, TILE), jnp.float32)
    state = (jnp.int32(0), table[0, START], table[0, STOP], jnp.float32(0.0), [zero] * 3)
    state = lax.while_loop(lambda s: s[0] < HEAD - STEP, step, state)
    for fetch in fetches[2:]:
        fetch.wait()
    lax.while_loop(lambda s: s[0] < shards, step, state)

    places = shards * 8
    ones = jnp.ones((8, TILE), jnp.float32)
    parts = []
    for c in range(3):
        left = lax.dot_general(
            ones,
            totals[c, 0:places, :],
            NT_DIMS,
            precision=EXACT,
            preferred_element_type=jnp.float32,
        )[0:1, :]
        for _ in range(3):
            near = left.astype(jnp.bfloat16)
            parts.append(near.astype(jnp.float32))
            left = left - parts[-1]
    parts = jnp.concatenate(parts + [jnp.zeros((7, places), jnp.float32)], axis=0)
    parts = parts.astype(jnp.bfloat16)
    place = lax.broadcasted_iota(jnp.int32, (places, TILE), 0)
    lane = lax.broadcasted_iota(jnp.int32, (places, TILE), 1)
    link = place >> 3
    slot = place & 7

    def collect(owner, node):
        pieces = []
        for chunk in range(leaf_count // TILE):
            row = owner * block + local + 6 * chunks + chunk
            parent = held_ref[pl.ds(row, 1), :].astype(jnp.int32) + leaf_count
            leaf = lane + chunk * TILE
            picked = jnp.where(node == leaf, 1.0, 0.0) + jnp.where(node == parent, 1.0, 0.0)
            sums = jnp.dot(
                parts, picked.astype(jnp.bfloat16), preferred_element_type=jnp.float32
            )
            pieces.append(
                jnp.concatenate(
                    [sums[3 * c : 3 * c + 1] + sums[3 * c + 1 : 3 * c + 2] + sums[3 * c + 2 : 3 * c + 3] for c in range(3)],
                    axis=0,
                )
            )
        return jnp.concatenate(pieces, axis=1)

    first_slot = jnp.where(late, split, 0)
    last_slot = jnp.where(late, per_peer, split)
    mine = (slot >= first_slot) & (slot < last_slot)
    result = collect(core, jnp.where(mine, link * per_peer + slot, -1))
    groups = out_ref.shape[0] // shard_c
    for group in range(groups):
        out_ref[group * shard_c + core] = result

    @pl.when(helps)
    def _():
        theirs = (slot >= per_peer) & (slot < per_peer + helped_count)
        node = jnp.where(theirs, link * per_peer + helped + slot - per_peer, -1)
        result = collect(1 - core, node)
        for group in range(groups):
            out_ref[group * shard_c + 1 - core] = result

    @pl.when(jnp.logical_not(helps))
    def _():
        for group in range(groups):
            out_ref[group * shard_c + 1 - core] = jnp.zeros((3, leaf_count), jnp.float32)


def gather_call(where, everything, sizes, groups, node_count, leaf_count):
    shards = sizes[0] * sizes[1] * sizes[2]
    return pl.pallas_call(
        functools.partial(
            gather_kernel, sizes=sizes, node_count=node_count, leaf_count=leaf_count
        ),
        out_shape=jax.ShapeDtypeStruct((groups * sizes[2], 3, leaf_count), jnp.float32),
        in_specs=[
            pl.BlockSpec(memory_space=pltpu.SMEM),
            pl.BlockSpec(memory_space=pltpu.VMEM),
        ],
        out_specs=pl.BlockSpec(memory_space=pltpu.VMEM),
        scratch_shapes=[
            pltpu.VMEM(((2 * shards + 1) * SOURCE, TILE), jnp.float32),
            pltpu.VMEM((6, node_count + 16, TILE), jnp.float32),
            pltpu.VMEM((6, (shards + 8) * 8, TILE), jnp.float32),
            pltpu.VMEM((3, (shards + 8) * 8, TILE), jnp.float32),
            pltpu.VMEM((2, shards + 8, TILE), jnp.int32),
            pltpu.SMEM((shards + 8, 2 * TILE), jnp.int32),
            pltpu.SemaphoreType.DMA((2, 2)),
        ],
        compiler_params=pltpu.CompilerParams(vmem_limit_bytes=40 * 1024 * 1024),
        name="gather",
    )(where, everything)


def body(
    leaf_emit,
    leaf_albedo,
    leaf_radiosity,
    leaf_area,
    parent_index,
    node_position,
    node_angles,
    block_receiver,
    block_source,
    block_count,
):
    leaf_count = leaf_area.shape[0]
    node_count = node_position.shape[1]
    sizes = tuple(lax.axis_size(axis) for axis in DEV)
    groups = lax.axis_size("grp")
    vmem = pl.BlockSpec(memory_space=pltpu.VMEM)
    own_rows = 8 * node_count // TILE
    held, local = pl.pallas_call(
        pack_kernel,
        out_shape=(
            jax.ShapeDtypeStruct((sizes[0], PACK // 4, 4, TILE), jnp.float32),
            jax.ShapeDtypeStruct((own_rows // 4, 4, TILE), jnp.float32),
        ),
        in_specs=[vmem] * 8,
        out_specs=(vmem, vmem),
        name="pack",
    )(
        leaf_radiosity,
        leaf_area[None, :],
        parent_index[None, :],
        node_position,
        node_angles,
        block_receiver,
        block_source,
        block_count,
    )
    held = lax.all_to_all(held, DEV[0], 0, 0, tiled=True).reshape(-1, 4, TILE)
    held = lax.all_to_all(
        jnp.broadcast_to(held[None], (sizes[1], *held.shape)), DEV[1], 0, 0, tiled=True
    )
    held = jnp.concatenate([held.reshape(-1, 4, TILE), local], axis=0)
    held = lax.all_to_all(
        jnp.broadcast_to(held[None], (sizes[2], *held.shape)), DEV[2], 0, 0, tiled=True
    )
    where = lax.axis_index(DEV).astype(jnp.int32).reshape(1)
    partial = gather_call(where, held.reshape(-1, TILE), sizes, groups, node_count, leaf_count)
    gathered = lax.all_to_all(partial, ("grp", DEV[2]), 0, 0, tiled=True).sum(axis=0)
    return leaf_emit + leaf_albedo * gathered


def solution(mesh):
    split = Mesh(
        mesh.devices.reshape(mesh.shape["grp"], 16, 4, 2), ("grp", "dev_0", "dev_1", "dev_2")
    )
    placed = (
        P(None, DEV),
        P(None, DEV),
        P(None, DEV),
        P(DEV),
        P(DEV),
        P(None, DEV),
        P(None, DEV),
        P("grp", DEV),
        P("grp", DEV),
        P("grp", DEV),
    )
    return jax.shard_map(body, mesh=split, in_specs=placed, out_specs=P(None, DEV), check_vma=False)
```

```python
import functools
import math

import jax
import jax.numpy as jnp
from jax import lax
from jax.experimental import pallas as pl
from jax.experimental.pallas import tpu as pltpu
from jax.sharding import Mesh
from jax.sharding import PartitionSpec as P

TILE = 128
DEV = ("dev_0", "dev_1", "dev_2")
QUAD = 4
QUADS = 40
STEP = 4
PACK = 20
FIELDS = 9
SOURCE = 16
OFFSETS = 248
SHIFT = 1 << 13
CHUNK = 512
EXACT = lax.Precision.HIGHEST
NT_DIMS = (((1,), (1,)), ((), ()))


def lane_rows(array):
    return [array[:, at : at + TILE] for at in range(0, array.shape[1], TILE)]


def pack_kernel(
    radiosity, area, parent, position, angles, receiver, source, count, pack_out, local_out
):
    leaf_count = area.shape[1]
    node_count = position.shape[1]
    cluster_count = node_count - leaf_count
    azimuth = angles[0:1, :]
    elevation = angles[1:2, :]
    cos_e = jnp.cos(elevation)
    nodes = [position[a : a + 1, :] for a in range(3)]
    nodes += [jnp.cos(azimuth) * cos_e, jnp.sin(azimuth) * cos_e, jnp.sin(elevation)]
    clusters = lax.broadcasted_iota(jnp.int32, (cluster_count, leaf_count), 0)
    onehot = (clusters == parent[...]).astype(jnp.float32)
    leaf_area = area[...]
    values = jnp.concatenate(
        [leaf_area, radiosity[...] * leaf_area, jnp.zeros((4, leaf_count), jnp.float32)], axis=0
    )
    sums = lax.dot_general(
        values, onehot, NT_DIMS, precision=EXACT, preferred_element_type=jnp.float32
    )
    cluster_area = sums[0:1, :]
    cluster_radiosity = sums[1:4, :] / cluster_area
    scale = cluster_area * (-1.0 / math.pi)
    slots = receiver.shape[1]
    tiles = lax.broadcasted_iota(jnp.int32, (8, slots), 0)
    lanes = lax.broadcasted_iota(jnp.int32, (8, slots), 1)
    live = lanes < count[...]
    member = jnp.where((tiles == receiver[...]) & live, 1.0, 0.0)
    before = (
        lax.broadcasted_iota(jnp.int32, (slots, slots), 0)
        < lax.broadcasted_iota(jnp.int32, (slots, slots), 1)
    ).astype(jnp.float32)
    place = jnp.dot(member, before, preferred_element_type=jnp.float32)
    held = jnp.sum(member, axis=1, keepdims=True)
    quads = jnp.broadcast_to(jnp.floor((held + (QUAD - 1)) * (1.0 / QUAD)), (8, slots))
    first = jnp.zeros((8, slots), jnp.float32)
    for t in range(7):
        first = first + jnp.where(tiles > t, quads[t : t + 1, :], 0.0)
    quad = jnp.floor(place * (1.0 / QUAD))
    turn = place - quad * QUAD
    spot = jnp.sum(member * (first + quad + turn * QUADS), axis=0, keepdims=True)
    alive = jnp.sum(member, axis=0, keepdims=True)
    spot = jnp.where(alive > 0.0, spot, -1.0).astype(jnp.int32)
    to_spot = (lax.broadcasted_iota(jnp.int32, (2 * slots, slots), 0) == spot).astype(jnp.float32)
    entries = jnp.broadcast_to((source[...] + 1).astype(jnp.float32), (8, slots))
    ordered = lax.dot_general(entries, to_spot, NT_DIMS, preferred_element_type=jnp.float32)
    offsets = jnp.sum(
        jnp.where(lanes == OFFSETS - TILE + tiles, first, 0.0), axis=0, keepdims=True
    )
    rows = []
    for half in range(cluster_count // TILE):
        cols = slice(half * TILE, half * TILE + TILE)
        at = slice(leaf_count + half * TILE, leaf_count + half * TILE + TILE)
        rows += [nodes[a][:, at] for a in range(3)]
        rows += [nodes[a][:, at] * scale[:, cols] for a in range(3, 6)]
        rows += [cluster_radiosity[c : c + 1, cols] for c in range(3)]
    rows += [ordered[0:1, :TILE], ordered[0:1, TILE:] + offsets]
    for piece in range(PACK // 4):
        part = jnp.concatenate(rows[piece * 4 : piece * 4 + 4], axis=0)
        for peer in range(pack_out.shape[0]):
            pack_out[peer, piece] = part
    local = [row for field in nodes for row in lane_rows(field)]
    local += lane_rows(parent[...].astype(jnp.float32))
    local += [jnp.zeros((1, TILE), jnp.float32)] * (local_out.shape[0] * 4 - len(local))
    for piece in range(len(local) // 4):
        local_out[piece] = jnp.concatenate(local[piece * 4 : piece * 4 + 4], axis=0)


def gather_kernel(
    where_ref,
    own_ref,
    other_ref,
    emit_ref,
    albedo_ref,
    out_ref,
    emit_out,
    albedo_out,
    sources,
    dense,
    receivers,
    totals,
    table_vmem,
    table,
    sem,
    *,
    sizes,
    node_count,
    leaf_count,
):
    shard_z, shard_y, shard_c = sizes
    shards = shard_z * shard_y * shard_c
    tiles = 2 * shards
    per_c = shard_y * shard_z
    per_peer = node_count // shards
    chunks = node_count // TILE
    blocks = (own_ref, other_ref)
    emit_out[...] = emit_ref[...]
    albedo_out[...] = albedo_ref[...]
    local = per_c * PACK
    here = where_ref[0]
    core = here & (shard_c - 1)

    def tile_of(shard):
        low = shard * per_peer // TILE
        high = (shard * per_peer + per_peer - 1) // TILE
        split = jnp.where(high > low, high * TILE - shard * per_peer, per_peer)
        late = split * 2 < per_peer
        return jnp.where(late, high, low), split, late

    tile, split, late = tile_of(here)
    partner = here ^ 1
    _, partner_split, partner_late = tile_of(partner)
    helps = partner_split < per_peer
    helped = jnp.where(partner_late, 0, partner_split)
    helped_count = jnp.where(partner_late, partner_split, per_peer - partner_split)

    def list_rows(at):
        return jnp.concatenate(
            [ref[pl.ds(at, per_c, stride=PACK), :] for ref in blocks], axis=0
        )

    low = list_rows(2 * FIELDS)
    high = list_rows(2 * FIELDS + 1)
    lane = lax.broadcasted_iota(jnp.int32, (shards, TILE), 1)
    arrival = lax.broadcasted_iota(jnp.int32, (shards, TILE), 0)
    first = jnp.sum(jnp.where(lane == OFFSETS - TILE + tile, high, 0.0), axis=1, keepdims=True)
    last = jnp.sum(jnp.where(lane == OFFSETS - TILE + tile + 1, high, 0.0), axis=1, keepdims=True)
    count = jnp.broadcast_to(last - first, (shards, TILE))
    upto = jnp.dot(
        (lane <= arrival).astype(jnp.bfloat16),
        count.astype(jnp.bfloat16),
        preferred_element_type=jnp.float32,
    )
    ahead = upto - count
    shift = first - ahead + SHIFT
    coarse = jnp.floor(shift * (1.0 / TILE))
    high = jnp.where(lane < OFFSETS - TILE, high, 0.0)
    extras = (arrival.astype(jnp.float32), coarse, shift - coarse * TILE, first)
    for n, extra in enumerate(extras):
        high = jnp.where(lane == OFFSETS - TILE + n, extra, high)
    listed = jnp.concatenate([low, high], axis=1).astype(jnp.bfloat16)

    def lay_out(chunk):
        spot = lax.broadcasted_iota(jnp.int32, (1, CHUNK), 1) + chunk * CHUNK
        place = spot.astype(jnp.float32)
        chosen = jnp.concatenate(
            [
                jnp.where((ahead <= part) & (part < upto), 1.0, 0.0)
                for part in lane_rows(place)
            ],
            axis=1,
        ).astype(jnp.bfloat16)
        found = lax.dot_general(
            listed, chosen, (((0,), (0,)), ((), ())), preferred_element_type=jnp.float32
        )
        owner = found[OFFSETS : OFFSETS + 1, :].astype(jnp.int32)
        quad = found[OFFSETS + 1 : OFFSETS + 2, :] * TILE + found[OFFSETS + 2 : OFFSETS + 3, :]
        quad = quad - SHIFT + place
        goes_on = jnp.where(quad > found[OFFSETS + 3 : OFFSETS + 4, :], 1, 0)
        quads = lax.broadcasted_iota(jnp.int32, (QUADS, CHUNK), 0).astype(jnp.float32)
        match = quads == quad
        entries = jnp.concatenate(
            [
                jnp.sum(
                    jnp.where(match, found[u * QUADS : (u + 1) * QUADS, :], 0.0),
                    axis=0,
                    keepdims=True,
                )
                for u in range(QUAD)
            ],
            axis=0,
        ).astype(jnp.int32)
        source = entries - 1
        giver = source >> 1
        came = (
            ((giver & (shard_c - 1)) ^ core) * per_c
            + ((giver >> (shard_c.bit_length() - 1)) & (shard_y - 1)) * shard_z
            + (giver >> ((shard_c * shard_y).bit_length() - 1))
        )
        rows = jnp.where(entries == 0, tiles, came * 2 + (source & 1)) * SOURCE
        link = (
            (owner & (shard_z - 1)) * (shard_y * shard_c)
            + ((owner >> (shard_z.bit_length() - 1)) & (shard_y - 1)) * shard_c
            + ((owner >> (per_c.bit_length() - 1)) ^ core)
        )
        total = jnp.concatenate([upto[shards - 1 : shards, :]] * (CHUNK // TILE), axis=1)
        total = total.astype(jnp.int32)
        link = jnp.where(spot < total, link, shards) * 8
        table_vmem[...] = jnp.concatenate(
            [rows, link, goes_on, total, jnp.zeros((1, CHUNK), jnp.int32)], axis=0
        )
        return pltpu.make_async_copy(table_vmem, table, sem)

    fetch = lay_out(0)
    fetch.start()

    for c, ref in enumerate(blocks):
        for half in range(2):
            base = half * FIELDS
            rows = [ref[pl.ds(base + f, per_c, stride=PACK), :] for f in range(FIELDS)]
            length = jnp.sqrt(rows[3] * rows[3] + rows[4] * rows[4] + rows[5] * rows[5])
            rows += [length * math.pi, length]
            for f, row in enumerate(rows):
                at = c * per_c * 2 * SOURCE + half * SOURCE + f
                sources[pl.ds(at, per_c, stride=2 * SOURCE), :] = row
    blank = lax.broadcasted_iota(jnp.int32, (SOURCE, TILE), 0) >= FIELDS
    sources[tiles * SOURCE : (tiles + 1) * SOURCE, :] = blank.astype(jnp.float32)

    def spread(ref):
        for chunk in range(chunks):
            turned = ref[pl.ds(local + chunk, 8, stride=chunks), :].T
            for field in range(6):
                dense[field, 8 + chunk * TILE : 8 + (chunk + 1) * TILE, :] = jnp.broadcast_to(
                    turned[:, field : field + 1], (TILE, TILE)
                )

    for field in range(6):
        dense[field, 0:8, :] = jnp.zeros((8, TILE), jnp.float32)
        dense[field, 8 + node_count : 16 + node_count, :] = jnp.zeros((8, TILE), jnp.float32)
        receivers[field, shards * 8 : (shards + 8) * 8, :] = jnp.zeros((64, TILE), jnp.float32)
    spread(own_ref)

    def settle(link, carry):
        for field in range(6):
            receivers[field, pl.ds(pl.multiple_of(link * 8, 8), 8), :] = dense[
                field, pl.ds(8 + link * per_peer, 8), :
            ]
        return carry

    lax.fori_loop(0, shards, settle, 0, unroll=8)

    @pl.when(helps)
    def _():
        spread(other_ref)
        keep = lax.broadcasted_iota(jnp.int32, (8, TILE), 0) < per_peer

        def join(link, carry):
            for field in range(6):
                rows = pl.ds(pl.multiple_of(link * 8, 8), 8)
                theirs = dense[field, pl.ds(8 + link * per_peer + helped - per_peer, 8), :]
                receivers[field, rows, :] = jnp.where(keep, receivers[field, rows, :], theirs)
            return carry

        lax.fori_loop(0, shards, join, 0, unroll=4)

    for c in range(3):
        totals[c, :, :] = jnp.zeros(((shards + 8) * 8, TILE), jnp.float32)

    def step(turn, acc):
        for n in range(STEP):
            spot = turn * STEP + n
            at = pl.ds(pl.multiple_of(table[QUAD, spot], 8), 8)
            keep = jnp.where(table[QUAD + 1, spot] > 0, 1.0, 0.0)
            rec = [receivers[field, at, :] for field in range(6)]
            acc = [a * keep for a in acc]
            for u in range(QUAD):
                row = pl.multiple_of(table[u, spot], SOURCE)
                src = [sources[pl.ds(row + f, 1), :] for f in range(FIELDS + 2)]
                d = [src[a] - rec[a] for a in range(3)]
                r2 = d[0] * d[0] + d[1] * d[1] + d[2] * d[2]
                toward = rec[3] * d[0] + rec[4] * d[1] + rec[5] * d[2]
                back = src[3] * d[0] + src[4] * d[1] + src[5] * d[2]
                top = jnp.maximum(toward, 0.0) * jnp.maximum(back, 0.0)
                factor = top / ((r2 + src[9]) * (r2 + src[10]))
                acc = [acc[c] + factor * src[6 + c] for c in range(3)]
            for c in range(3):
                totals[c, at, :] = acc[c]
        return acc

    def work_off(chunk, acc):
        held = jnp.clip(table[QUAD + 2, 0] - chunk * CHUNK, 0, CHUNK)
        return lax.fori_loop(0, (held + STEP - 1) // STEP, step, acc)

    def next_chunk(chunk, acc):
        again = lay_out(chunk)
        again.start()
        again.wait()
        return work_off(chunk, acc)

    zero = jnp.zeros((8, TILE), jnp.float32)
    fetch.wait()
    acc = work_off(0, [zero] * 3)
    lax.fori_loop(1, (table[QUAD + 2, 0] + CHUNK - 1) // CHUNK, next_chunk, acc)

    places = shards * 8
    ones = jnp.ones((8, TILE), jnp.float32)
    parts = []
    for c in range(3):
        left = lax.dot_general(
            ones,
            totals[c, 0:places, :],
            NT_DIMS,
            precision=EXACT,
            preferred_element_type=jnp.float32,
        )[0:1, :]
        for _ in range(3):
            near = left.astype(jnp.bfloat16)
            parts.append(near.astype(jnp.float32))
            left = left - parts[-1]
    parts = jnp.concatenate(parts + [jnp.zeros((7, places), jnp.float32)], axis=0)
    parts = parts.astype(jnp.bfloat16)
    place = lax.broadcasted_iota(jnp.int32, (places, TILE), 0)
    lane = lax.broadcasted_iota(jnp.int32, (places, TILE), 1)
    link = place >> 3
    slot = place & 7

    def collect(ref, node):
        pieces = []
        for chunk in range(leaf_count // TILE):
            parent = ref[pl.ds(local + 6 * chunks + chunk, 1), :].astype(jnp.int32) + leaf_count
            leaf = lane + chunk * TILE
            picked = jnp.where(node == leaf, 1.0, 0.0) + jnp.where(node == parent, 1.0, 0.0)
            sums = jnp.dot(
                parts, picked.astype(jnp.bfloat16), preferred_element_type=jnp.float32
            )
            pieces.append(
                jnp.concatenate(
                    [sums[3 * c : 3 * c + 1] + sums[3 * c + 1 : 3 * c + 2] + sums[3 * c + 2 : 3 * c + 3] for c in range(3)],
                    axis=0,
                )
            )
        return jnp.concatenate(pieces, axis=1)

    first_slot = jnp.where(late, split, 0)
    last_slot = jnp.where(late, per_peer, split)
    mine = (slot >= first_slot) & (slot < last_slot)
    result = collect(own_ref, jnp.where(mine, link * per_peer + slot, -1))
    groups = out_ref.shape[0] // shard_c
    for group in range(groups):
        out_ref[group * shard_c + core] = result

    @pl.when(helps)
    def _():
        theirs = (slot >= per_peer) & (slot < per_peer + helped_count)
        node = jnp.where(theirs, link * per_peer + helped + slot - per_peer, -1)
        result = collect(other_ref, node)
        for group in range(groups):
            out_ref[group * shard_c + 1 - core] = result

    @pl.when(jnp.logical_not(helps))
    def _():
        for group in range(groups):
            out_ref[group * shard_c + 1 - core] = jnp.zeros((3, leaf_count), jnp.float32)


def gather_call(where, own, other, emit, albedo, sizes, groups, node_count, leaf_count):
    shards = sizes[0] * sizes[1] * sizes[2]
    return pl.pallas_call(
        functools.partial(
            gather_kernel, sizes=sizes, node_count=node_count, leaf_count=leaf_count
        ),
        out_shape=(
            jax.ShapeDtypeStruct((groups * sizes[2], 3, leaf_count), jnp.float32),
            jax.ShapeDtypeStruct(emit.shape, jnp.float32),
            jax.ShapeDtypeStruct(albedo.shape, jnp.float32),
        ),
        in_specs=[pl.BlockSpec(memory_space=pltpu.SMEM)]
        + [pl.BlockSpec(memory_space=pltpu.VMEM)] * 4,
        out_specs=(pl.BlockSpec(memory_space=pltpu.VMEM),) * 3,
        scratch_shapes=[
            pltpu.VMEM(((2 * shards + 1) * SOURCE, TILE), jnp.float32),
            pltpu.VMEM((6, node_count + 16, TILE), jnp.float32),
            pltpu.VMEM((6, (shards + 8) * 8, TILE), jnp.float32),
            pltpu.VMEM((3, (shards + 8) * 8, TILE), jnp.float32),
            pltpu.VMEM((8, CHUNK), jnp.int32),
            pltpu.SMEM((8, CHUNK), jnp.int32),
            pltpu.SemaphoreType.DMA(()),
        ],
        compiler_params=pltpu.CompilerParams(vmem_limit_bytes=20 * 1024 * 1024),
        name="gather",
    )(where, own, other, emit, albedo)


def body(
    leaf_emit,
    leaf_albedo,
    leaf_radiosity,
    leaf_area,
    parent_index,
    node_position,
    node_angles,
    block_receiver,
    block_source,
    block_count,
):
    leaf_count = leaf_area.shape[0]
    node_count = node_position.shape[1]
    sizes = tuple(lax.axis_size(axis) for axis in DEV)
    groups = lax.axis_size("grp")
    vmem = pl.BlockSpec(memory_space=pltpu.VMEM)
    own_rows = 8 * node_count // TILE
    held, local = pl.pallas_call(
        pack_kernel,
        out_shape=(
            jax.ShapeDtypeStruct((sizes[0], PACK // 4, 4, TILE), jnp.float32),
            jax.ShapeDtypeStruct((own_rows // 4, 4, TILE), jnp.float32),
        ),
        in_specs=[vmem] * 8,
        out_specs=(vmem, vmem),
        name="pack",
    )(
        leaf_radiosity,
        leaf_area[None, :],
        parent_index[None, :],
        node_position,
        node_angles,
        block_receiver,
        block_source,
        block_count,
    )
    held = lax.all_to_all(held, DEV[0], 0, 0, tiled=True).reshape(-1, 4, TILE)
    held = lax.all_to_all(
        jnp.broadcast_to(held[None], (sizes[1], *held.shape)), DEV[1], 0, 0, tiled=True
    )
    held = jnp.concatenate([held.reshape(-1, 4, TILE), local], axis=0)
    other = lax.ppermute(held, DEV[2], [(0, 1), (1, 0)])
    where = lax.axis_index(DEV).astype(jnp.int32).reshape(1)
    partial, emit, albedo = gather_call(
        where,
        held.reshape(-1, TILE),
        other.reshape(-1, TILE),
        leaf_emit,
        leaf_albedo,
        sizes,
        groups,
        node_count,
        leaf_count,
    )
    gathered = lax.all_to_all(partial, ("grp", DEV[2]), 0, 0, tiled=True).sum(axis=0)
    return emit + albedo * gathered


def solution(mesh):
    split = Mesh(
        mesh.devices.reshape(mesh.shape["grp"], 16, 4, 2), ("grp", "dev_0", "dev_1", "dev_2")
    )
    placed = (
        P(None, DEV),
        P(None, DEV),
        P(None, DEV),
        P(DEV),
        P(DEV),
        P(None, DEV),
        P(None, DEV),
        P("grp", DEV),
        P("grp", DEV),
        P("grp", DEV),
    )
    return jax.shard_map(body, mesh=split, in_specs=placed, out_specs=P(None, DEV), check_vma=False)
```

```python
import functools
import math

import jax
import jax.numpy as jnp
from jax import lax
from jax.experimental import pallas as pl
from jax.experimental.pallas import tpu as pltpu
from jax.sharding import Mesh
from jax.sharding import PartitionSpec as P

TILE = 128
DEV = ("dev_0", "dev_1", "dev_2")
QUAD = 4
QUADS = 40
STEP = 4
PACK = 20
FIELDS = 9
SOURCE = 16
OFFSETS = 248
SHIFT = 1 << 13
CHUNK = 512
NT_DIMS = (((1,), (1,)), ((), ()))


def lane_rows(array):
    return [array[:, at : at + TILE] for at in range(0, array.shape[1], TILE)]


def terms(array, count):
    parts = []
    for _ in range(count):
        parts.append(array.astype(jnp.bfloat16).astype(jnp.float32))
        array = array - parts[-1]
    return parts


def pack_kernel(
    radiosity, area, parent, position, angles, receiver, source, count, pack_out, local_out
):
    leaf_count = area.shape[1]
    node_count = position.shape[1]
    cluster_count = node_count - leaf_count
    azimuth = angles[0:1, :]
    elevation = angles[1:2, :]
    cos_e = jnp.cos(elevation)
    nodes = [position[a : a + 1, :] for a in range(3)]
    nodes += [jnp.cos(azimuth) * cos_e, jnp.sin(azimuth) * cos_e, jnp.sin(elevation)]
    clusters = lax.broadcasted_iota(jnp.int32, (cluster_count, leaf_count), 0)
    onehot = (clusters == parent[...]).astype(jnp.bfloat16)
    leaf_area = area[...]
    values = jnp.concatenate(
        [leaf_area, radiosity[...] * leaf_area, jnp.zeros((4, leaf_count), jnp.float32)], axis=0
    )
    sums = lax.dot_general(
        jnp.concatenate(terms(values, 3), axis=0).astype(jnp.bfloat16),
        onehot,
        NT_DIMS,
        preferred_element_type=jnp.float32,
    )
    sums = sums[0:8, :] + sums[8:16, :] + sums[16:24, :]
    cluster_area = sums[0:1, :]
    cluster_radiosity = sums[1:4, :] / cluster_area
    scale = cluster_area * (-1.0 / math.pi)
    slots = receiver.shape[1]
    tiles = lax.broadcasted_iota(jnp.int32, (8, slots), 0)
    lanes = lax.broadcasted_iota(jnp.int32, (8, slots), 1)
    live = lanes < count[...]
    member = jnp.where((tiles == receiver[...]) & live, 1.0, 0.0)
    before = (
        lax.broadcasted_iota(jnp.int32, (slots, slots), 0)
        < lax.broadcasted_iota(jnp.int32, (slots, slots), 1)
    ).astype(jnp.bfloat16)
    place = jnp.dot(member.astype(jnp.bfloat16), before, preferred_element_type=jnp.float32)
    held = jnp.sum(member, axis=1, keepdims=True)
    quads = jnp.broadcast_to(jnp.floor((held + (QUAD - 1)) * (1.0 / QUAD)), (8, slots))
    first = jnp.zeros((8, slots), jnp.float32)
    for t in range(7):
        first = first + jnp.where(tiles > t, quads[t : t + 1, :], 0.0)
    quad = jnp.floor(place * (1.0 / QUAD))
    turn = place - quad * QUAD
    spot = jnp.sum(member * (first + quad + turn * QUADS), axis=0, keepdims=True)
    alive = jnp.sum(member, axis=0, keepdims=True)
    spot = jnp.where(alive > 0.0, spot, -1.0).astype(jnp.int32)
    to_spot = (lax.broadcasted_iota(jnp.int32, (2 * slots, slots), 0) == spot).astype(jnp.bfloat16)
    entries = jnp.broadcast_to((source[...] + 1).astype(jnp.float32), (8, slots))
    entries = entries.astype(jnp.bfloat16)
    ordered = lax.dot_general(entries, to_spot, NT_DIMS, preferred_element_type=jnp.float32)
    offsets = jnp.sum(
        jnp.where(lanes == OFFSETS - TILE + tiles, first, 0.0), axis=0, keepdims=True
    )
    rows = []
    for half in range(cluster_count // TILE):
        cols = slice(half * TILE, half * TILE + TILE)
        at = slice(leaf_count + half * TILE, leaf_count + half * TILE + TILE)
        rows += [nodes[a][:, at] for a in range(3)]
        rows += [nodes[a][:, at] * scale[:, cols] for a in range(3, 6)]
        rows += [cluster_radiosity[c : c + 1, cols] for c in range(3)]
    rows += [ordered[0:1, :TILE], ordered[0:1, TILE:] + offsets]
    for piece in range(PACK // 4):
        part = jnp.concatenate(rows[piece * 4 : piece * 4 + 4], axis=0)
        for peer in range(pack_out.shape[0]):
            pack_out[peer, piece] = part
    local = [row for field in nodes for row in lane_rows(field)]
    local += lane_rows(parent[...].astype(jnp.float32))
    local += [jnp.zeros((1, TILE), jnp.float32)] * (local_out.shape[0] * 4 - len(local))
    for piece in range(len(local) // 4):
        local_out[piece] = jnp.concatenate(local[piece * 4 : piece * 4 + 4], axis=0)


def gather_kernel(
    where_ref,
    own_ref,
    other_ref,
    emit_ref,
    albedo_ref,
    out_ref,
    emit_out,
    albedo_out,
    sources,
    dense,
    receivers,
    totals,
    table_vmem,
    table,
    sem,
    *,
    sizes,
    node_count,
    leaf_count,
):
    shard_z, shard_y, shard_c = sizes
    shards = shard_z * shard_y * shard_c
    tiles = 2 * shards
    per_c = shard_y * shard_z
    per_peer = node_count // shards
    chunks = node_count // TILE
    blocks = (own_ref, other_ref)
    emit_out[...] = emit_ref[...]
    albedo_out[...] = albedo_ref[...]
    local = per_c * PACK
    here = where_ref[0]
    core = here & (shard_c - 1)

    def tile_of(shard):
        low = shard * per_peer // TILE
        high = (shard * per_peer + per_peer - 1) // TILE
        split = jnp.where(high > low, high * TILE - shard * per_peer, per_peer)
        late = split * 2 < per_peer
        return jnp.where(late, high, low), split, late

    tile, split, late = tile_of(here)
    partner = here ^ 1
    _, partner_split, partner_late = tile_of(partner)
    helps = partner_split < per_peer
    helped = jnp.where(partner_late, 0, partner_split)
    helped_count = jnp.where(partner_late, partner_split, per_peer - partner_split)

    def list_rows(at):
        return jnp.concatenate(
            [ref[pl.ds(at, per_c, stride=PACK), :] for ref in blocks], axis=0
        )

    low = list_rows(2 * FIELDS)
    high = list_rows(2 * FIELDS + 1)
    lane = lax.broadcasted_iota(jnp.int32, (shards, TILE), 1)
    arrival = lax.broadcasted_iota(jnp.int32, (shards, TILE), 0)
    first = jnp.sum(jnp.where(lane == OFFSETS - TILE + tile, high, 0.0), axis=1, keepdims=True)
    last = jnp.sum(jnp.where(lane == OFFSETS - TILE + tile + 1, high, 0.0), axis=1, keepdims=True)
    count = jnp.broadcast_to(last - first, (shards, TILE))
    upto = jnp.dot(
        (lane <= arrival).astype(jnp.bfloat16),
        count.astype(jnp.bfloat16),
        preferred_element_type=jnp.float32,
    )
    ahead = upto - count
    shift = first - ahead + SHIFT
    coarse = jnp.floor(shift * (1.0 / TILE))
    high = jnp.where(lane < OFFSETS - TILE, high, 0.0)
    extras = (arrival.astype(jnp.float32), coarse, shift - coarse * TILE, first)
    for n, extra in enumerate(extras):
        high = jnp.where(lane == OFFSETS - TILE + n, extra, high)
    listed = jnp.concatenate([low, high], axis=1).astype(jnp.bfloat16)

    def lay_out(chunk):
        spot = lax.broadcasted_iota(jnp.int32, (1, CHUNK), 1) + chunk * CHUNK
        place = spot.astype(jnp.float32)
        chosen = jnp.concatenate(
            [
                jnp.where((ahead <= part) & (part < upto), 1.0, 0.0)
                for part in lane_rows(place)
            ],
            axis=1,
        ).astype(jnp.bfloat16)
        found = lax.dot_general(
            listed, chosen, (((0,), (0,)), ((), ())), preferred_element_type=jnp.float32
        )
        owner = found[OFFSETS : OFFSETS + 1, :].astype(jnp.int32)
        quad = found[OFFSETS + 1 : OFFSETS + 2, :] * TILE + found[OFFSETS + 2 : OFFSETS + 3, :]
        quad = quad - SHIFT + place
        goes_on = jnp.where(quad > found[OFFSETS + 3 : OFFSETS + 4, :], 1, 0)
        quads = lax.broadcasted_iota(jnp.int32, (QUADS, CHUNK), 0).astype(jnp.float32)
        match = quads == quad
        entries = jnp.concatenate(
            [
                jnp.sum(
                    jnp.where(match, found[u * QUADS : (u + 1) * QUADS, :], 0.0),
                    axis=0,
                    keepdims=True,
                )
                for u in range(QUAD)
            ],
            axis=0,
        ).astype(jnp.int32)
        source = entries - 1
        giver = source >> 1
        came = (
            ((giver & (shard_c - 1)) ^ core) * per_c
            + ((giver >> (shard_c.bit_length() - 1)) & (shard_y - 1)) * shard_z
            + (giver >> ((shard_c * shard_y).bit_length() - 1))
        )
        rows = jnp.where(entries == 0, tiles, came * 2 + (source & 1)) * SOURCE
        link = (
            (owner & (shard_z - 1)) * (shard_y * shard_c)
            + ((owner >> (shard_z.bit_length() - 1)) & (shard_y - 1)) * shard_c
            + ((owner >> (per_c.bit_length() - 1)) ^ core)
        )
        total = jnp.concatenate([upto[shards - 1 : shards, :]] * (CHUNK // TILE), axis=1)
        total = total.astype(jnp.int32)
        link = jnp.where(spot < total, link, shards) * 8
        table_vmem[...] = jnp.concatenate(
            [rows, link, goes_on, total, jnp.zeros((1, CHUNK), jnp.int32)], axis=0
        )
        return pltpu.make_async_copy(table_vmem, table, sem)

    fetch = lay_out(0)
    fetch.start()

    for c, ref in enumerate(blocks):
        for half in range(2):
            base = half * FIELDS
            rows = [ref[pl.ds(base + f, per_c, stride=PACK), :] for f in range(FIELDS)]
            length = jnp.sqrt(rows[3] * rows[3] + rows[4] * rows[4] + rows[5] * rows[5])
            rows += [length * math.pi, length]
            for f, row in enumerate(rows):
                at = c * per_c * 2 * SOURCE + half * SOURCE + f
                sources[pl.ds(at, per_c, stride=2 * SOURCE), :] = row
    blank = lax.broadcasted_iota(jnp.int32, (SOURCE, TILE), 0) >= FIELDS
    sources[tiles * SOURCE : (tiles + 1) * SOURCE, :] = blank.astype(jnp.float32)

    def spread(ref):
        for chunk in range(chunks):
            turned = ref[pl.ds(local + chunk, 8, stride=chunks), :].T
            for field in range(6):
                dense[field, 8 + chunk * TILE : 8 + (chunk + 1) * TILE, :] = jnp.broadcast_to(
                    turned[:, field : field + 1], (TILE, TILE)
                )

    for field in range(6):
        dense[field, 0:8, :] = jnp.zeros((8, TILE), jnp.float32)
        dense[field, 8 + node_count : 16 + node_count, :] = jnp.zeros((8, TILE), jnp.float32)
        receivers[field, shards * 8 : (shards + 8) * 8, :] = jnp.zeros((64, TILE), jnp.float32)
    spread(own_ref)

    def settle(link, carry):
        for field in range(6):
            receivers[field, pl.ds(pl.multiple_of(link * 8, 8), 8), :] = dense[
                field, pl.ds(8 + link * per_peer, 8), :
            ]
        return carry

    lax.fori_loop(0, shards, settle, 0, unroll=8)

    @pl.when(helps)
    def _():
        spread(other_ref)
        keep = lax.broadcasted_iota(jnp.int32, (8, TILE), 0) < per_peer

        def join(link, carry):
            for field in range(6):
                rows = pl.ds(pl.multiple_of(link * 8, 8), 8)
                theirs = dense[field, pl.ds(8 + link * per_peer + helped - per_peer, 8), :]
                receivers[field, rows, :] = jnp.where(keep, receivers[field, rows, :], theirs)
            return carry

        lax.fori_loop(0, shards, join, 0, unroll=4)

    for c in range(3):
        totals[c, :, :] = jnp.zeros(((shards + 8) * 8, TILE), jnp.float32)

    def step(turn, acc):
        for n in range(STEP):
            spot = turn * STEP + n
            at = pl.ds(pl.multiple_of(table[QUAD, spot], 8), 8)
            keep = jnp.where(table[QUAD + 1, spot] > 0, 1.0, 0.0)
            rec = [receivers[field, at, :] for field in range(6)]
            acc = [a * keep for a in acc]
            for u in range(QUAD):
                row = pl.multiple_of(table[u, spot], SOURCE)
                src = [sources[pl.ds(row + f, 1), :] for f in range(FIELDS + 2)]
                d = [src[a] - rec[a] for a in range(3)]
                r2 = d[0] * d[0] + d[1] * d[1] + d[2] * d[2]
                toward = rec[3] * d[0] + rec[4] * d[1] + rec[5] * d[2]
                back = src[3] * d[0] + src[4] * d[1] + src[5] * d[2]
                top = jnp.maximum(toward, 0.0) * jnp.maximum(back, 0.0)
                factor = top / ((r2 + src[9]) * (r2 + src[10]))
                acc = [acc[c] + factor * src[6 + c] for c in range(3)]
            for c in range(3):
                totals[c, at, :] = acc[c]
        return acc

    def work_off(chunk, acc):
        held = jnp.clip(table[QUAD + 2, 0] - chunk * CHUNK, 0, CHUNK)
        return lax.fori_loop(0, (held + STEP - 1) // STEP, step, acc)

    def next_chunk(chunk, acc):
        again = lay_out(chunk)
        again.start()
        again.wait()
        return work_off(chunk, acc)

    zero = jnp.zeros((8, TILE), jnp.float32)
    fetch.wait()
    acc = work_off(0, [zero] * 3)
    lax.fori_loop(1, (table[QUAD + 2, 0] + CHUNK - 1) // CHUNK, next_chunk, acc)

    places = shards * 8
    band = lax.broadcasted_iota(jnp.int32, (TILE, TILE), 1)
    sums = jnp.zeros((places, TILE), jnp.float32)
    for c in range(3):
        to_band = (band == c).astype(jnp.bfloat16)
        for part in terms(totals[c, 0:places, :], 2):
            sums = sums + jnp.dot(
                part.astype(jnp.bfloat16), to_band, preferred_element_type=jnp.float32
            )
    parts = jnp.concatenate(terms(sums.T[0:8, :], 2), axis=0).astype(jnp.bfloat16)
    place = lax.broadcasted_iota(jnp.int32, (places, TILE), 0)
    lane = lax.broadcasted_iota(jnp.int32, (places, TILE), 1)
    link = place >> 3
    slot = place & 7

    def collect(ref, node):
        pieces = []
        for chunk in range(leaf_count // TILE):
            parent = ref[pl.ds(local + 6 * chunks + chunk, 1), :].astype(jnp.int32) + leaf_count
            leaf = lane + chunk * TILE
            picked = jnp.where(node == leaf, 1.0, 0.0) + jnp.where(node == parent, 1.0, 0.0)
            sums = jnp.dot(
                parts, picked.astype(jnp.bfloat16), preferred_element_type=jnp.float32
            )
            pieces.append(sums[0:3, :] + sums[8:11, :])
        return jnp.concatenate(pieces, axis=1)

    first_slot = jnp.where(late, split, 0)
    last_slot = jnp.where(late, per_peer, split)
    mine = (slot >= first_slot) & (slot < last_slot)
    result = collect(own_ref, jnp.where(mine, link * per_peer + slot, -1))
    groups = out_ref.shape[0] // shard_c
    for group in range(groups):
        out_ref[group * shard_c + core] = result

    @pl.when(helps)
    def _():
        theirs = (slot >= per_peer) & (slot < per_peer + helped_count)
        node = jnp.where(theirs, link * per_peer + helped + slot - per_peer, -1)
        result = collect(other_ref, node)
        for group in range(groups):
            out_ref[group * shard_c + 1 - core] = result

    @pl.when(jnp.logical_not(helps))
    def _():
        for group in range(groups):
            out_ref[group * shard_c + 1 - core] = jnp.zeros((3, leaf_count), jnp.float32)


def gather_call(where, own, other, emit, albedo, sizes, groups, node_count, leaf_count):
    shards = sizes[0] * sizes[1] * sizes[2]
    return pl.pallas_call(
        functools.partial(
            gather_kernel, sizes=sizes, node_count=node_count, leaf_count=leaf_count
        ),
        out_shape=(
            jax.ShapeDtypeStruct((groups * sizes[2], 3, leaf_count), jnp.float32),
            jax.ShapeDtypeStruct(emit.shape, jnp.float32),
            jax.ShapeDtypeStruct(albedo.shape, jnp.float32),
        ),
        in_specs=[pl.BlockSpec(memory_space=pltpu.SMEM)]
        + [pl.BlockSpec(memory_space=pltpu.VMEM)] * 4,
        out_specs=(pl.BlockSpec(memory_space=pltpu.VMEM),) * 3,
        scratch_shapes=[
            pltpu.VMEM(((2 * shards + 1) * SOURCE, TILE), jnp.float32),
            pltpu.VMEM((6, node_count + 16, TILE), jnp.float32),
            pltpu.VMEM((6, (shards + 8) * 8, TILE), jnp.float32),
            pltpu.VMEM((3, (shards + 8) * 8, TILE), jnp.float32),
            pltpu.VMEM((8, CHUNK), jnp.int32),
            pltpu.SMEM((8, CHUNK), jnp.int32),
            pltpu.SemaphoreType.DMA(()),
        ],
        compiler_params=pltpu.CompilerParams(vmem_limit_bytes=20 * 1024 * 1024),
        name="gather",
    )(where, own, other, emit, albedo)


def body(
    leaf_emit,
    leaf_albedo,
    leaf_radiosity,
    leaf_area,
    parent_index,
    node_position,
    node_angles,
    block_receiver,
    block_source,
    block_count,
):
    leaf_count = leaf_area.shape[0]
    node_count = node_position.shape[1]
    sizes = tuple(lax.axis_size(axis) for axis in DEV)
    groups = lax.axis_size("grp")
    vmem = pl.BlockSpec(memory_space=pltpu.VMEM)
    own_rows = 8 * node_count // TILE
    held, local = pl.pallas_call(
        pack_kernel,
        out_shape=(
            jax.ShapeDtypeStruct((sizes[0], PACK // 4, 4, TILE), jnp.float32),
            jax.ShapeDtypeStruct((own_rows // 4, 4, TILE), jnp.float32),
        ),
        in_specs=[vmem] * 8,
        out_specs=(vmem, vmem),
        name="pack",
    )(
        leaf_radiosity,
        leaf_area[None, :],
        parent_index[None, :],
        node_position,
        node_angles,
        block_receiver,
        block_source,
        block_count,
    )
    held = lax.all_to_all(held, DEV[0], 0, 0, tiled=True).reshape(-1, 4, TILE)
    held = lax.all_to_all(
        jnp.broadcast_to(held[None], (sizes[1], *held.shape)), DEV[1], 0, 0, tiled=True
    )
    held = jnp.concatenate([held.reshape(-1, 4, TILE), local], axis=0)
    other = lax.ppermute(held, DEV[2], [(0, 1), (1, 0)])
    where = lax.axis_index(DEV).astype(jnp.int32).reshape(1)
    partial, emit, albedo = gather_call(
        where,
        held.reshape(-1, TILE),
        other.reshape(-1, TILE),
        leaf_emit,
        leaf_albedo,
        sizes,
        groups,
        node_count,
        leaf_count,
    )
    gathered = lax.all_to_all(partial, ("grp", DEV[2]), 0, 0, tiled=True).sum(axis=0)
    return emit + albedo * gathered


def solution(mesh):
    split = Mesh(
        mesh.devices.reshape(mesh.shape["grp"], 16, 4, 2), ("grp", "dev_0", "dev_1", "dev_2")
    )
    placed = (
        P(None, DEV),
        P(None, DEV),
        P(None, DEV),
        P(DEV),
        P(DEV),
        P(None, DEV),
        P(None, DEV),
        P("grp", DEV),
        P("grp", DEV),
        P("grp", DEV),
    )
    return jax.shard_map(body, mesh=split, in_specs=placed, out_specs=P(None, DEV), check_vma=False)
```

```python
import functools
import math

import jax
import jax.numpy as jnp
from jax import lax
from jax.experimental import pallas as pl
from jax.experimental.pallas import tpu as pltpu
from jax.sharding import Mesh
from jax.sharding import PartitionSpec as P

TILE = 128
DEV = ("dev_0", "dev_1", "dev_2")
RUN = 3
RUNS = 48
STEP = 8
PACK = 20
FIELDS = 9
SOURCE = 16
OFFSETS = 248
SHIFT = 1 << 13
CHUNK = 640
NT_DIMS = (((1,), (1,)), ((), ()))


def lane_rows(array):
    return [array[:, at : at + TILE] for at in range(0, array.shape[1], TILE)]


def terms(array, count):
    parts = []
    for _ in range(count):
        parts.append(array.astype(jnp.bfloat16).astype(jnp.float32))
        array = array - parts[-1]
    return parts


def pack_kernel(
    radiosity, area, parent, position, angles, receiver, source, count, pack_out, local_out
):
    leaf_count = area.shape[1]
    node_count = position.shape[1]
    cluster_count = node_count - leaf_count
    sines = jnp.sin(angles[...])
    cosines = jnp.cos(angles[...])
    cos_e = cosines[1:2, :]
    nodes = [position[a : a + 1, :] for a in range(3)]
    nodes += [cosines[0:1, :] * cos_e, sines[0:1, :] * cos_e, sines[1:2, :]]
    clusters = lax.broadcasted_iota(jnp.int32, (cluster_count, leaf_count), 0)
    onehot = (clusters == parent[...]).astype(jnp.bfloat16)
    leaf_area = area[...]
    values = jnp.concatenate(
        [leaf_area, radiosity[...] * leaf_area, jnp.zeros((4, leaf_count), jnp.float32)], axis=0
    )
    sums = lax.dot_general(
        jnp.concatenate(terms(values, 3), axis=0).astype(jnp.bfloat16),
        onehot,
        NT_DIMS,
        preferred_element_type=jnp.float32,
    )
    sums = sums[0:8, :] + sums[8:16, :] + sums[16:24, :]
    cluster_area = sums[0:1, :]
    cluster_radiosity = sums[1:4, :] / cluster_area
    scale = cluster_area * (-1.0 / math.pi)
    slots = receiver.shape[1]
    tiles = lax.broadcasted_iota(jnp.int32, (8, slots), 0)
    lanes = lax.broadcasted_iota(jnp.int32, (8, slots), 1)
    live = lanes < count[...]
    member = jnp.where((tiles == receiver[...]) & live, 1.0, 0.0)
    before = (
        lax.broadcasted_iota(jnp.int32, (slots, slots), 0)
        < lax.broadcasted_iota(jnp.int32, (slots, slots), 1)
    ).astype(jnp.bfloat16)
    place = jnp.dot(member.astype(jnp.bfloat16), before, preferred_element_type=jnp.float32)
    held = jnp.sum(member, axis=1, keepdims=True)
    runs = jnp.broadcast_to(jnp.floor((held + (RUN - 0.5)) * (1.0 / RUN)), (8, slots))
    first = jnp.zeros((8, slots), jnp.float32)
    for t in range(7):
        first = first + jnp.where(tiles > t, runs[t : t + 1, :], 0.0)
    run = jnp.floor((place + 0.5) * (1.0 / RUN))
    turn = place - run * RUN
    spot = jnp.sum(member * (first + run + turn * RUNS), axis=0, keepdims=True)
    alive = jnp.sum(member, axis=0, keepdims=True)
    spot = jnp.where(alive > 0.0, spot, -1.0).astype(jnp.int32)
    to_spot = (lax.broadcasted_iota(jnp.int32, (2 * slots, slots), 0) == spot).astype(jnp.bfloat16)
    entries = jnp.broadcast_to((source[...] + 1).astype(jnp.float32), (8, slots))
    entries = entries.astype(jnp.bfloat16)
    ordered = lax.dot_general(entries, to_spot, NT_DIMS, preferred_element_type=jnp.float32)
    offsets = jnp.sum(
        jnp.where(lanes == OFFSETS - TILE + tiles, first, 0.0), axis=0, keepdims=True
    )
    rows = []
    for half in range(cluster_count // TILE):
        cols = slice(half * TILE, half * TILE + TILE)
        at = slice(leaf_count + half * TILE, leaf_count + half * TILE + TILE)
        rows += [nodes[a][:, at] for a in range(3)]
        rows += [nodes[a][:, at] * scale[:, cols] for a in range(3, 6)]
        rows += [cluster_radiosity[c : c + 1, cols] for c in range(3)]
    rows += [ordered[0:1, :TILE], ordered[0:1, TILE:] + offsets]
    for piece in range(PACK // 4):
        part = jnp.concatenate(rows[piece * 4 : piece * 4 + 4], axis=0)
        for peer in range(pack_out.shape[0]):
            pack_out[peer, piece] = part
    local = [row for field in nodes for row in lane_rows(field)]
    local += lane_rows(parent[...].astype(jnp.float32))
    local += [jnp.zeros((1, TILE), jnp.float32)] * (local_out.shape[0] * 4 - len(local))
    for piece in range(len(local) // 4):
        local_out[piece] = jnp.concatenate(local[piece * 4 : piece * 4 + 4], axis=0)


def gather_kernel(
    where_ref,
    own_ref,
    other_ref,
    emit_ref,
    albedo_ref,
    out_ref,
    emit_out,
    albedo_out,
    sources,
    dense,
    receivers,
    totals,
    table_vmem,
    table,
    sem,
    *,
    sizes,
    node_count,
    leaf_count,
):
    shard_z, shard_y, shard_c = sizes
    shards = shard_z * shard_y * shard_c
    tiles = 2 * shards
    per_c = shard_y * shard_z
    per_peer = node_count // shards
    chunks = node_count // TILE
    blocks = (own_ref, other_ref)
    emit_out[...] = emit_ref[...]
    albedo_out[...] = albedo_ref[...]
    local = per_c * PACK
    here = where_ref[0]
    core = here & (shard_c - 1)

    def tile_of(shard):
        low = shard * per_peer // TILE
        high = (shard * per_peer + per_peer - 1) // TILE
        split = jnp.where(high > low, high * TILE - shard * per_peer, per_peer)
        late = split * 2 < per_peer
        return jnp.where(late, high, low), split, late

    tile, split, late = tile_of(here)
    partner = here ^ 1
    _, partner_split, partner_late = tile_of(partner)
    helps = partner_split < per_peer
    helped = jnp.where(partner_late, 0, partner_split)
    helped_count = jnp.where(partner_late, partner_split, per_peer - partner_split)

    def list_rows(at):
        return jnp.concatenate(
            [ref[pl.ds(at, per_c, stride=PACK), :] for ref in blocks], axis=0
        )

    low = list_rows(2 * FIELDS)
    high = list_rows(2 * FIELDS + 1)
    lane = lax.broadcasted_iota(jnp.int32, (shards, TILE), 1)
    arrival = lax.broadcasted_iota(jnp.int32, (shards, TILE), 0)
    first = jnp.sum(jnp.where(lane == OFFSETS - TILE + tile, high, 0.0), axis=1, keepdims=True)
    last = jnp.sum(jnp.where(lane == OFFSETS - TILE + tile + 1, high, 0.0), axis=1, keepdims=True)
    count = jnp.broadcast_to(last - first, (shards, TILE))
    upto = jnp.dot(
        (lane <= arrival).astype(jnp.bfloat16),
        count.astype(jnp.bfloat16),
        preferred_element_type=jnp.float32,
    )
    ahead = upto - count
    shift = first - ahead + SHIFT
    coarse = jnp.floor(shift * (1.0 / TILE))
    high = jnp.where(lane < OFFSETS - TILE, high, 0.0)
    extras = (arrival.astype(jnp.float32), coarse, shift - coarse * TILE, first)
    for n, extra in enumerate(extras):
        high = jnp.where(lane == OFFSETS - TILE + n, extra, high)
    listed = jnp.concatenate([low, high], axis=1).astype(jnp.bfloat16)

    def lay_out(chunk):
        spot = lax.broadcasted_iota(jnp.int32, (1, CHUNK), 1) + chunk * CHUNK
        place = spot.astype(jnp.float32)
        chosen = jnp.concatenate(
            [
                jnp.where((ahead <= part) & (part < upto), 1.0, 0.0)
                for part in lane_rows(place)
            ],
            axis=1,
        ).astype(jnp.bfloat16)
        found = lax.dot_general(
            listed, chosen, (((0,), (0,)), ((), ())), preferred_element_type=jnp.float32
        )
        owner = found[OFFSETS : OFFSETS + 1, :].astype(jnp.int32)
        run = found[OFFSETS + 1 : OFFSETS + 2, :] * TILE + found[OFFSETS + 2 : OFFSETS + 3, :]
        run = run - SHIFT + place
        goes_on = jnp.where(run > found[OFFSETS + 3 : OFFSETS + 4, :], 1, 0)
        runs = lax.broadcasted_iota(jnp.int32, (RUNS, CHUNK), 0).astype(jnp.float32)
        match = runs == run
        entries = jnp.concatenate(
            [
                jnp.sum(
                    jnp.where(match, found[u * RUNS : (u + 1) * RUNS, :], 0.0),
                    axis=0,
                    keepdims=True,
                )
                for u in range(RUN)
            ],
            axis=0,
        ).astype(jnp.int32)
        source = entries - 1
        giver = source >> 1
        came = (
            ((giver & (shard_c - 1)) ^ core) * per_c
            + ((giver >> (shard_c.bit_length() - 1)) & (shard_y - 1)) * shard_z
            + (giver >> ((shard_c * shard_y).bit_length() - 1))
        )
        rows = jnp.where(entries == 0, tiles, came * 2 + (source & 1)) * SOURCE
        link = (
            (owner & (shard_z - 1)) * (shard_y * shard_c)
            + ((owner >> (shard_z.bit_length() - 1)) & (shard_y - 1)) * shard_c
            + ((owner >> (per_c.bit_length() - 1)) ^ core)
        )
        total = jnp.concatenate([upto[shards - 1 : shards, :]] * (CHUNK // TILE), axis=1)
        total = total.astype(jnp.int32)
        link = jnp.where(spot < total, link, shards) * 8
        table_vmem[...] = jnp.concatenate(
            [rows, link, goes_on, total, jnp.zeros((5 - RUN, CHUNK), jnp.int32)], axis=0
        )
        return pltpu.make_async_copy(table_vmem, table, sem)

    fetch = lay_out(0)
    fetch.start()

    for c, ref in enumerate(blocks):
        for half in range(2):
            base = half * FIELDS
            rows = [ref[pl.ds(base + f, per_c, stride=PACK), :] for f in range(FIELDS)]
            length = jnp.sqrt(rows[3] * rows[3] + rows[4] * rows[4] + rows[5] * rows[5])
            rows += [length * math.pi, length]
            for f, row in enumerate(rows):
                at = c * per_c * 2 * SOURCE + half * SOURCE + f
                sources[pl.ds(at, per_c, stride=2 * SOURCE), :] = row
    blank = lax.broadcasted_iota(jnp.int32, (SOURCE, TILE), 0) >= FIELDS
    sources[tiles * SOURCE : (tiles + 1) * SOURCE, :] = blank.astype(jnp.float32)

    def spread(ref):
        for chunk in range(chunks):
            turned = ref[pl.ds(local + chunk, 8, stride=chunks), :].T
            for field in range(6):
                dense[field, 8 + chunk * TILE : 8 + (chunk + 1) * TILE, :] = jnp.broadcast_to(
                    turned[:, field : field + 1], (TILE, TILE)
                )

    for field in range(6):
        dense[field, 0:8, :] = jnp.zeros((8, TILE), jnp.float32)
        dense[field, 8 + node_count : 16 + node_count, :] = jnp.zeros((8, TILE), jnp.float32)
        receivers[field, shards * 8 : (shards + 8) * 8, :] = jnp.zeros((64, TILE), jnp.float32)
    spread(own_ref)

    def settle(link, carry):
        for field in range(6):
            receivers[field, pl.ds(pl.multiple_of(link * 8, 8), 8), :] = dense[
                field, pl.ds(8 + link * per_peer, 8), :
            ]
        return carry

    lax.fori_loop(0, shards, settle, 0, unroll=8)

    @pl.when(helps)
    def _():
        spread(other_ref)
        keep = lax.broadcasted_iota(jnp.int32, (8, TILE), 0) < per_peer

        def join(link, carry):
            for field in range(6):
                rows = pl.ds(pl.multiple_of(link * 8, 8), 8)
                theirs = dense[field, pl.ds(8 + link * per_peer + helped - per_peer, 8), :]
                receivers[field, rows, :] = jnp.where(keep, receivers[field, rows, :], theirs)
            return carry

        lax.fori_loop(0, shards, join, 0, unroll=4)

    for c in range(3):
        totals[c, :, :] = jnp.zeros(((shards + 8) * 8, TILE), jnp.float32)

    def step(turn, acc):
        for n in range(STEP):
            spot = turn * STEP + n
            at = pl.ds(pl.multiple_of(table[RUN, spot], 8), 8)
            keep = jnp.where(table[RUN + 1, spot] > 0, 1.0, 0.0)
            rec = [receivers[field, at, :] for field in range(6)]
            acc = [a * keep for a in acc]
            for u in range(RUN):
                row = pl.multiple_of(table[u, spot], SOURCE)
                src = [sources[pl.ds(row + f, 1), :] for f in range(FIELDS + 2)]
                d = [src[a] - rec[a] for a in range(3)]
                r2 = d[0] * d[0] + d[1] * d[1] + d[2] * d[2]
                toward = rec[3] * d[0] + rec[4] * d[1] + rec[5] * d[2]
                back = src[3] * d[0] + src[4] * d[1] + src[5] * d[2]
                top = jnp.maximum(toward, 0.0) * jnp.maximum(back, 0.0)
                factor = top / ((r2 + src[9]) * (r2 + src[10]))
                acc = [acc[c] + factor * src[6 + c] for c in range(3)]
            for c in range(3):
                totals[c, at, :] = acc[c]
        return acc

    def work_off(chunk, acc):
        held = jnp.clip(table[RUN + 2, 0] - chunk * CHUNK, 0, CHUNK)
        return lax.fori_loop(0, (held + STEP - 1) // STEP, step, acc)

    def next_chunk(chunk, acc):
        again = lay_out(chunk)
        again.start()
        again.wait()
        return work_off(chunk, acc)

    zero = jnp.zeros((8, TILE), jnp.float32)
    fetch.wait()
    acc = work_off(0, [zero] * 3)
    lax.fori_loop(1, (table[RUN + 2, 0] + CHUNK - 1) // CHUNK, next_chunk, acc)

    places = shards * 8
    band = lax.broadcasted_iota(jnp.int32, (TILE, TILE), 1)
    sums = jnp.zeros((places, TILE), jnp.float32)
    for c in range(3):
        to_band = (band == c).astype(jnp.bfloat16)
        whole = totals[c, 0:places, :]
        near = whole.astype(jnp.bfloat16)
        rest = (whole - near.astype(jnp.float32)).astype(jnp.bfloat16)
        for part in (near, rest):
            sums = sums + jnp.dot(part, to_band, preferred_element_type=jnp.float32)
    parts = jnp.concatenate(terms(sums.T[0:8, :], 2), axis=0).astype(jnp.bfloat16)
    place = lax.broadcasted_iota(jnp.int32, (places, TILE), 0)
    lane = lax.broadcasted_iota(jnp.int32, (places, TILE), 1)
    link = place >> 3
    slot = place & 7

    def collect(ref, node):
        pieces = []
        for chunk in range(leaf_count // TILE):
            parent = ref[pl.ds(local + 6 * chunks + chunk, 1), :].astype(jnp.int32) + leaf_count
            leaf = lane + chunk * TILE
            picked = jnp.where((node == leaf) | (node == parent), 1.0, 0.0)
            sums = jnp.dot(
                parts, picked.astype(jnp.bfloat16), preferred_element_type=jnp.float32
            )
            pieces.append(sums[0:3, :] + sums[8:11, :])
        return jnp.concatenate(pieces, axis=1)

    first_slot = jnp.where(late, split, 0)
    last_slot = jnp.where(late, per_peer, split)
    mine = (slot >= first_slot) & (slot < last_slot)
    result = collect(own_ref, jnp.where(mine, link * per_peer + slot, -1))
    groups = out_ref.shape[0] // shard_c
    for group in range(groups):
        out_ref[group * shard_c + core] = result

    @pl.when(helps)
    def _():
        theirs = (slot >= per_peer) & (slot < per_peer + helped_count)
        node = jnp.where(theirs, link * per_peer + helped + slot - per_peer, -1)
        result = collect(other_ref, node)
        for group in range(groups):
            out_ref[group * shard_c + 1 - core] = result

    @pl.when(jnp.logical_not(helps))
    def _():
        for group in range(groups):
            out_ref[group * shard_c + 1 - core] = jnp.zeros((3, leaf_count), jnp.float32)


def gather_call(where, own, other, emit, albedo, sizes, groups, node_count, leaf_count):
    shards = sizes[0] * sizes[1] * sizes[2]
    return pl.pallas_call(
        functools.partial(
            gather_kernel, sizes=sizes, node_count=node_count, leaf_count=leaf_count
        ),
        out_shape=(
            jax.ShapeDtypeStruct((groups * sizes[2], 3, leaf_count), jnp.float32),
            jax.ShapeDtypeStruct(emit.shape, jnp.float32),
            jax.ShapeDtypeStruct(albedo.shape, jnp.float32),
        ),
        in_specs=[pl.BlockSpec(memory_space=pltpu.SMEM)]
        + [pl.BlockSpec(memory_space=pltpu.VMEM)] * 4,
        out_specs=(pl.BlockSpec(memory_space=pltpu.VMEM),) * 3,
        scratch_shapes=[
            pltpu.VMEM(((2 * shards + 1) * SOURCE, TILE), jnp.float32),
            pltpu.VMEM((6, node_count + 16, TILE), jnp.float32),
            pltpu.VMEM((6, (shards + 8) * 8, TILE), jnp.float32),
            pltpu.VMEM((3, (shards + 8) * 8, TILE), jnp.float32),
            pltpu.VMEM((8, CHUNK), jnp.int32),
            pltpu.SMEM((8, CHUNK), jnp.int32),
            pltpu.SemaphoreType.DMA(()),
        ],
        compiler_params=pltpu.CompilerParams(vmem_limit_bytes=20 * 1024 * 1024),
        name="gather",
    )(where, own, other, emit, albedo)


def body(
    leaf_emit,
    leaf_albedo,
    leaf_radiosity,
    leaf_area,
    parent_index,
    node_position,
    node_angles,
    block_receiver,
    block_source,
    block_count,
):
    leaf_count = leaf_area.shape[0]
    node_count = node_position.shape[1]
    sizes = tuple(lax.axis_size(axis) for axis in DEV)
    groups = lax.axis_size("grp")
    vmem = pl.BlockSpec(memory_space=pltpu.VMEM)
    own_rows = 8 * node_count // TILE
    held, local = pl.pallas_call(
        pack_kernel,
        out_shape=(
            jax.ShapeDtypeStruct((sizes[0], PACK // 4, 4, TILE), jnp.float32),
            jax.ShapeDtypeStruct((own_rows // 4, 4, TILE), jnp.float32),
        ),
        in_specs=[vmem] * 8,
        out_specs=(vmem, vmem),
        name="pack",
    )(
        leaf_radiosity,
        leaf_area[None, :],
        parent_index[None, :],
        node_position,
        node_angles,
        block_receiver,
        block_source,
        block_count,
    )
    held = lax.all_to_all(held, DEV[0], 0, 0, tiled=True).reshape(-1, 4, TILE)
    held = lax.all_to_all(
        jnp.broadcast_to(held[None], (sizes[1], *held.shape)), DEV[1], 0, 0, tiled=True
    )
    held = jnp.concatenate([held.reshape(-1, 4, TILE), local], axis=0)
    other = lax.ppermute(held, DEV[2], [(0, 1), (1, 0)])
    where = lax.axis_index(DEV).astype(jnp.int32).reshape(1)
    partial, emit, albedo = gather_call(
        where,
        held.reshape(-1, TILE),
        other.reshape(-1, TILE),
        leaf_emit,
        leaf_albedo,
        sizes,
        groups,
        node_count,
        leaf_count,
    )
    gathered = lax.all_to_all(partial, ("grp", DEV[2]), 0, 0, tiled=True).sum(axis=0)
    return emit + albedo * gathered


def solution(mesh):
    split = Mesh(
        mesh.devices.reshape(mesh.shape["grp"], 16, 4, 2), ("grp", "dev_0", "dev_1", "dev_2")
    )
    placed = (
        P(None, DEV),
        P(None, DEV),
        P(None, DEV),
        P(DEV),
        P(DEV),
        P(None, DEV),
        P(None, DEV),
        P("grp", DEV),
        P("grp", DEV),
        P("grp", DEV),
    )
    return jax.shard_map(body, mesh=split, in_specs=placed, out_specs=P(None, DEV), check_vma=False)
```

```python
import functools
import math

import jax
import jax.numpy as jnp
from jax import lax
from jax.experimental import pallas as pl
from jax.experimental.pallas import tpu as pltpu
from jax.sharding import Mesh
from jax.sharding import PartitionSpec as P

TILE = 128
DEV = ("dev_0", "dev_1", "dev_2")
RUN = 3
RUNS = 48
STEP = 16
PACK = 20
FIELDS = 9
SOURCE = 16
OFFSETS = 248
SHIFT = 1 << 13
CHUNK = 640
NT_DIMS = (((1,), (1,)), ((), ()))


def lane_rows(array):
    return [array[:, at : at + TILE] for at in range(0, array.shape[1], TILE)]


def terms(array, count):
    parts = []
    for _ in range(count):
        parts.append(array.astype(jnp.bfloat16).astype(jnp.float32))
        array = array - parts[-1]
    return parts


def pack_kernel(
    radiosity, area, parent, position, angles, receiver, source, count, pack_out, local_out
):
    leaf_count = area.shape[1]
    node_count = position.shape[1]
    cluster_count = node_count - leaf_count
    sines = jnp.sin(angles[...])
    cosines = jnp.cos(angles[...])
    cos_e = cosines[1:2, :]
    nodes = [position[a : a + 1, :] for a in range(3)]
    nodes += [cosines[0:1, :] * cos_e, sines[0:1, :] * cos_e, sines[1:2, :]]
    clusters = lax.broadcasted_iota(jnp.int32, (cluster_count, leaf_count), 0)
    onehot = (clusters == parent[...]).astype(jnp.bfloat16)
    leaf_area = area[...]
    values = jnp.concatenate(
        [leaf_area, radiosity[...] * leaf_area, jnp.zeros((4, leaf_count), jnp.float32)], axis=0
    )
    sums = lax.dot_general(
        jnp.concatenate(terms(values, 3), axis=0).astype(jnp.bfloat16),
        onehot,
        NT_DIMS,
        preferred_element_type=jnp.float32,
    )
    sums = sums[0:8, :] + sums[8:16, :] + sums[16:24, :]
    cluster_area = sums[0:1, :]
    cluster_radiosity = sums[1:4, :] / cluster_area
    scale = cluster_area * (-1.0 / math.pi)
    slots = receiver.shape[1]
    tiles = lax.broadcasted_iota(jnp.int32, (8, slots), 0)
    lanes = lax.broadcasted_iota(jnp.int32, (8, slots), 1)
    live = lanes < count[...]
    member = jnp.where((tiles == receiver[...]) & live, 1.0, 0.0)
    before = (
        lax.broadcasted_iota(jnp.int32, (slots, slots), 0)
        < lax.broadcasted_iota(jnp.int32, (slots, slots), 1)
    ).astype(jnp.bfloat16)
    place = jnp.dot(member.astype(jnp.bfloat16), before, preferred_element_type=jnp.float32)
    held = jnp.sum(member, axis=1, keepdims=True)
    runs = jnp.broadcast_to(jnp.floor((held + (RUN - 0.5)) * (1.0 / RUN)), (8, slots))
    first = jnp.zeros((8, slots), jnp.float32)
    for t in range(7):
        first = first + jnp.where(tiles > t, runs[t : t + 1, :], 0.0)
    run = jnp.floor((place + 0.5) * (1.0 / RUN))
    turn = place - run * RUN
    spot = jnp.sum(member * (first + run + turn * RUNS), axis=0, keepdims=True)
    alive = jnp.sum(member, axis=0, keepdims=True)
    spot = jnp.where(alive > 0.0, spot, -1.0).astype(jnp.int32)
    to_spot = (lax.broadcasted_iota(jnp.int32, (2 * slots, slots), 0) == spot).astype(jnp.bfloat16)
    entries = jnp.broadcast_to((source[...] + 1).astype(jnp.float32), (8, slots))
    entries = entries.astype(jnp.bfloat16)
    ordered = lax.dot_general(entries, to_spot, NT_DIMS, preferred_element_type=jnp.float32)
    offsets = jnp.sum(
        jnp.where(lanes == OFFSETS - TILE + tiles, first, 0.0), axis=0, keepdims=True
    )
    rows = []
    for half in range(cluster_count // TILE):
        cols = slice(half * TILE, half * TILE + TILE)
        at = slice(leaf_count + half * TILE, leaf_count + half * TILE + TILE)
        rows += [nodes[a][:, at] for a in range(3)]
        rows += [nodes[a][:, at] * scale[:, cols] for a in range(3, 6)]
        rows += [cluster_radiosity[c : c + 1, cols] for c in range(3)]
    rows += [ordered[0:1, :TILE], ordered[0:1, TILE:] + offsets]
    for piece in range(PACK // 4):
        part = jnp.concatenate(rows[piece * 4 : piece * 4 + 4], axis=0)
        for peer in range(pack_out.shape[0]):
            pack_out[peer, piece] = part
    local = [row for field in nodes for row in lane_rows(field)]
    local += lane_rows(parent[...].astype(jnp.float32))
    local += [jnp.zeros((1, TILE), jnp.float32)] * (local_out.shape[0] * 4 - len(local))
    for piece in range(len(local) // 4):
        local_out[piece] = jnp.concatenate(local[piece * 4 : piece * 4 + 4], axis=0)


def gather_kernel(
    where_ref,
    own_ref,
    other_ref,
    emit_ref,
    albedo_ref,
    out_ref,
    emit_out,
    albedo_out,
    sources,
    dense,
    receivers,
    totals,
    table_vmem,
    table,
    sem,
    *,
    sizes,
    node_count,
    leaf_count,
):
    shard_z, shard_y, shard_c = sizes
    shards = shard_z * shard_y * shard_c
    tiles = 2 * shards
    per_c = shard_y * shard_z
    per_peer = node_count // shards
    chunks = node_count // TILE
    blocks = (own_ref, other_ref)
    emit_out[...] = emit_ref[...]
    albedo_out[...] = albedo_ref[...]
    local = per_c * PACK
    here = where_ref[0]
    core = here & (shard_c - 1)

    def tile_of(shard):
        low = shard * per_peer // TILE
        high = (shard * per_peer + per_peer - 1) // TILE
        split = jnp.where(high > low, high * TILE - shard * per_peer, per_peer)
        late = split * 2 < per_peer
        return jnp.where(late, high, low), split, late

    tile, split, late = tile_of(here)
    partner = here ^ 1
    _, partner_split, partner_late = tile_of(partner)
    helps = partner_split < per_peer
    helped = jnp.where(partner_late, 0, partner_split)
    helped_count = jnp.where(partner_late, partner_split, per_peer - partner_split)

    def list_rows(at):
        return jnp.concatenate(
            [ref[pl.ds(at, per_c, stride=PACK), :] for ref in blocks], axis=0
        )

    low = list_rows(2 * FIELDS)
    high = list_rows(2 * FIELDS + 1)
    lane = lax.broadcasted_iota(jnp.int32, (shards, TILE), 1)
    arrival = lax.broadcasted_iota(jnp.int32, (shards, TILE), 0)
    first = jnp.sum(jnp.where(lane == OFFSETS - TILE + tile, high, 0.0), axis=1, keepdims=True)
    last = jnp.sum(jnp.where(lane == OFFSETS - TILE + tile + 1, high, 0.0), axis=1, keepdims=True)
    count = jnp.broadcast_to(last - first, (shards, TILE))
    upto = jnp.dot(
        (lane <= arrival).astype(jnp.bfloat16),
        count.astype(jnp.bfloat16),
        preferred_element_type=jnp.float32,
    )
    ahead = upto - count
    shift = first - ahead + SHIFT
    coarse = jnp.floor(shift * (1.0 / TILE))
    high = jnp.where(lane < OFFSETS - TILE, high, 0.0)
    extras = (arrival.astype(jnp.float32), coarse, shift - coarse * TILE)
    for n, extra in enumerate(extras):
        high = jnp.where(lane == OFFSETS - TILE + n, extra, high)
    listed = jnp.concatenate([low, high], axis=1).astype(jnp.bfloat16)

    def lay_out(chunk):
        spot = lax.broadcasted_iota(jnp.int32, (1, CHUNK), 1) + chunk * CHUNK
        place = spot.astype(jnp.float32)
        chosen = jnp.concatenate(
            [
                jnp.where((ahead <= part) & (part < upto), 1.0, 0.0)
                for part in lane_rows(place)
            ],
            axis=1,
        ).astype(jnp.bfloat16)
        found = lax.dot_general(
            listed, chosen, (((0,), (0,)), ((), ())), preferred_element_type=jnp.float32
        )
        owner = found[OFFSETS : OFFSETS + 1, :].astype(jnp.int32)
        run = found[OFFSETS + 1 : OFFSETS + 2, :] * TILE + found[OFFSETS + 2 : OFFSETS + 3, :]
        run = run - SHIFT + place
        runs = lax.broadcasted_iota(jnp.int32, (RUNS, CHUNK), 0).astype(jnp.float32)
        match = runs == run
        entries = jnp.concatenate(
            [
                jnp.sum(
                    jnp.where(match, found[u * RUNS : (u + 1) * RUNS, :], 0.0),
                    axis=0,
                    keepdims=True,
                )
                for u in range(RUN)
            ],
            axis=0,
        ).astype(jnp.int32)
        source = entries - 1
        giver = source >> 1
        came = (
            ((giver & (shard_c - 1)) ^ core) * per_c
            + ((giver >> (shard_c.bit_length() - 1)) & (shard_y - 1)) * shard_z
            + (giver >> ((shard_c * shard_y).bit_length() - 1))
        )
        rows = jnp.where(entries == 0, tiles, came * 2 + (source & 1)) * SOURCE
        link = (
            (owner & (shard_z - 1)) * (shard_y * shard_c)
            + ((owner >> (shard_z.bit_length() - 1)) & (shard_y - 1)) * shard_c
            + ((owner >> (per_c.bit_length() - 1)) ^ core)
        )
        total = jnp.concatenate([upto[shards - 1 : shards, :]] * (CHUNK // TILE), axis=1)
        total = total.astype(jnp.int32)
        link = jnp.where(spot < total, link, shards) * 8
        table_vmem[...] = jnp.concatenate(
            [rows, link, total, jnp.zeros((6 - RUN, CHUNK), jnp.int32)], axis=0
        )
        return pltpu.make_async_copy(table_vmem, table, sem)

    fetch = lay_out(0)
    fetch.start()

    for c, ref in enumerate(blocks):
        for half in range(2):
            base = half * FIELDS
            rows = [ref[pl.ds(base + f, per_c, stride=PACK), :] for f in range(FIELDS)]
            length = jnp.sqrt(rows[3] * rows[3] + rows[4] * rows[4] + rows[5] * rows[5])
            rows += [length * math.pi, length]
            for f, row in enumerate(rows):
                at = c * per_c * 2 * SOURCE + half * SOURCE + f
                sources[pl.ds(at, per_c, stride=2 * SOURCE), :] = row
    blank = lax.broadcasted_iota(jnp.int32, (SOURCE, TILE), 0) >= FIELDS
    sources[tiles * SOURCE : (tiles + 1) * SOURCE, :] = blank.astype(jnp.float32)

    def spread(ref):
        for chunk in range(chunks):
            turned = ref[pl.ds(local + chunk, 8, stride=chunks), :].T
            for field in range(6):
                dense[field, 8 + chunk * TILE : 8 + (chunk + 1) * TILE, :] = jnp.broadcast_to(
                    turned[:, field : field + 1], (TILE, TILE)
                )

    for field in range(6):
        dense[field, 0:8, :] = jnp.zeros((8, TILE), jnp.float32)
        dense[field, 8 + node_count : 16 + node_count, :] = jnp.zeros((8, TILE), jnp.float32)
        receivers[field, shards * 8 : (shards + 8) * 8, :] = jnp.zeros((64, TILE), jnp.float32)
    spread(own_ref)

    def settle(link, carry):
        for field in range(6):
            receivers[field, pl.ds(pl.multiple_of(link * 8, 8), 8), :] = dense[
                field, pl.ds(8 + link * per_peer, 8), :
            ]
        return carry

    lax.fori_loop(0, shards, settle, 0, unroll=8)

    @pl.when(helps)
    def _():
        spread(other_ref)
        keep = lax.broadcasted_iota(jnp.int32, (8, TILE), 0) < per_peer

        def join(link, carry):
            for field in range(6):
                rows = pl.ds(pl.multiple_of(link * 8, 8), 8)
                theirs = dense[field, pl.ds(8 + link * per_peer + helped - per_peer, 8), :]
                receivers[field, rows, :] = jnp.where(keep, receivers[field, rows, :], theirs)
            return carry

        lax.fori_loop(0, shards, join, 0, unroll=4)

    for c in range(3):
        totals[c, :, :] = jnp.zeros(((shards + 8) * 8, TILE), jnp.float32)

    def step(turn, carry):
        for n in range(STEP):
            spot = turn * STEP + n
            at = pl.ds(pl.multiple_of(table[RUN, spot], 8), 8)
            rec = [receivers[field, at, :] for field in range(6)]
            acc = None
            for u in range(RUN):
                row = pl.multiple_of(table[u, spot], SOURCE)
                src = [sources[pl.ds(row + f, 1), :] for f in range(FIELDS + 2)]
                d = [src[a] - rec[a] for a in range(3)]
                r2 = d[0] * d[0] + d[1] * d[1] + d[2] * d[2]
                toward = rec[3] * d[0] + rec[4] * d[1] + rec[5] * d[2]
                back = src[3] * d[0] + src[4] * d[1] + src[5] * d[2]
                top = jnp.maximum(toward, 0.0) * jnp.maximum(back, 0.0)
                factor = top / ((r2 + src[9]) * (r2 + src[10]))
                more = [factor * src[6 + c] for c in range(3)]
                acc = more if acc is None else [acc[c] + more[c] for c in range(3)]
            for c in range(3):
                totals[c, at, :] = totals[c, at, :] + acc[c]
        return carry

    def work_off(chunk):
        held = jnp.clip(table[RUN + 1, 0] - chunk * CHUNK, 0, CHUNK)
        lax.fori_loop(0, (held + STEP - 1) // STEP, step, 0)

    def next_chunk(chunk, carry):
        again = lay_out(chunk)
        again.start()
        again.wait()
        work_off(chunk)
        return carry

    fetch.wait()
    work_off(0)
    lax.fori_loop(1, (table[RUN + 1, 0] + CHUNK - 1) // CHUNK, next_chunk, 0)

    places = shards * 8
    band = lax.broadcasted_iota(jnp.int32, (TILE, TILE), 1)
    sums = jnp.zeros((places, TILE), jnp.float32)
    for c in range(3):
        to_band = (band == c).astype(jnp.bfloat16)
        whole = totals[c, 0:places, :]
        near = whole.astype(jnp.bfloat16)
        rest = (whole - near.astype(jnp.float32)).astype(jnp.bfloat16)
        for part in (near, rest):
            sums = sums + jnp.dot(part, to_band, preferred_element_type=jnp.float32)
    parts = jnp.concatenate(terms(sums.T[0:8, :], 2), axis=0).astype(jnp.bfloat16)
    place = lax.broadcasted_iota(jnp.int32, (places, TILE), 0)
    lane = lax.broadcasted_iota(jnp.int32, (places, TILE), 1)
    link = place >> 3
    slot = place & 7

    def collect(ref, node):
        pieces = []
        for chunk in range(leaf_count // TILE):
            parent = ref[pl.ds(local + 6 * chunks + chunk, 1), :].astype(jnp.int32) + leaf_count
            leaf = lane + chunk * TILE
            picked = jnp.where((node == leaf) | (node == parent), 1.0, 0.0)
            sums = jnp.dot(
                parts, picked.astype(jnp.bfloat16), preferred_element_type=jnp.float32
            )
            pieces.append(sums[0:3, :] + sums[8:11, :])
        return jnp.concatenate(pieces, axis=1)

    first_slot = jnp.where(late, split, 0)
    last_slot = jnp.where(late, per_peer, split)
    mine = (slot >= first_slot) & (slot < last_slot)
    result = collect(own_ref, jnp.where(mine, link * per_peer + slot, -1))
    groups = out_ref.shape[0] // shard_c
    for group in range(groups):
        out_ref[group * shard_c + core] = result

    @pl.when(helps)
    def _():
        theirs = (slot >= per_peer) & (slot < per_peer + helped_count)
        node = jnp.where(theirs, link * per_peer + helped + slot - per_peer, -1)
        result = collect(other_ref, node)
        for group in range(groups):
            out_ref[group * shard_c + 1 - core] = result

    @pl.when(jnp.logical_not(helps))
    def _():
        for group in range(groups):
            out_ref[group * shard_c + 1 - core] = jnp.zeros((3, leaf_count), jnp.float32)


def gather_call(where, own, other, emit, albedo, sizes, groups, node_count, leaf_count):
    shards = sizes[0] * sizes[1] * sizes[2]
    return pl.pallas_call(
        functools.partial(
            gather_kernel, sizes=sizes, node_count=node_count, leaf_count=leaf_count
        ),
        out_shape=(
            jax.ShapeDtypeStruct((groups * sizes[2], 3, leaf_count), jnp.float32),
            jax.ShapeDtypeStruct(emit.shape, jnp.float32),
            jax.ShapeDtypeStruct(albedo.shape, jnp.float32),
        ),
        in_specs=[pl.BlockSpec(memory_space=pltpu.SMEM)]
        + [pl.BlockSpec(memory_space=pltpu.VMEM)] * 4,
        out_specs=(pl.BlockSpec(memory_space=pltpu.VMEM),) * 3,
        scratch_shapes=[
            pltpu.VMEM(((2 * shards + 1) * SOURCE, TILE), jnp.float32),
            pltpu.VMEM((6, node_count + 16, TILE), jnp.float32),
            pltpu.VMEM((6, (shards + 8) * 8, TILE), jnp.float32),
            pltpu.VMEM((3, (shards + 8) * 8, TILE), jnp.float32),
            pltpu.VMEM((8, CHUNK), jnp.int32),
            pltpu.SMEM((8, CHUNK), jnp.int32),
            pltpu.SemaphoreType.DMA(()),
        ],
        compiler_params=pltpu.CompilerParams(vmem_limit_bytes=20 * 1024 * 1024),
        name="gather",
    )(where, own, other, emit, albedo)


def body(
    leaf_emit,
    leaf_albedo,
    leaf_radiosity,
    leaf_area,
    parent_index,
    node_position,
    node_angles,
    block_receiver,
    block_source,
    block_count,
):
    leaf_count = leaf_area.shape[0]
    node_count = node_position.shape[1]
    sizes = tuple(lax.axis_size(axis) for axis in DEV)
    groups = lax.axis_size("grp")
    vmem = pl.BlockSpec(memory_space=pltpu.VMEM)
    own_rows = 8 * node_count // TILE
    held, local = pl.pallas_call(
        pack_kernel,
        out_shape=(
            jax.ShapeDtypeStruct((sizes[0], PACK // 4, 4, TILE), jnp.float32),
            jax.ShapeDtypeStruct((own_rows // 4, 4, TILE), jnp.float32),
        ),
        in_specs=[vmem] * 8,
        out_specs=(vmem, vmem),
        name="pack",
    )(
        leaf_radiosity,
        leaf_area[None, :],
        parent_index[None, :],
        node_position,
        node_angles,
        block_receiver,
        block_source,
        block_count,
    )
    held = lax.all_to_all(held, DEV[0], 0, 0, tiled=True).reshape(-1, 4, TILE)
    held = lax.all_to_all(
        jnp.broadcast_to(held[None], (sizes[1], *held.shape)), DEV[1], 0, 0, tiled=True
    )
    held = jnp.concatenate([held.reshape(-1, 4, TILE), local], axis=0)
    other = lax.ppermute(held, DEV[2], [(0, 1), (1, 0)])
    where = lax.axis_index(DEV).astype(jnp.int32).reshape(1)
    partial, emit, albedo = gather_call(
        where,
        held.reshape(-1, TILE),
        other.reshape(-1, TILE),
        leaf_emit,
        leaf_albedo,
        sizes,
        groups,
        node_count,
        leaf_count,
    )
    gathered = lax.all_to_all(partial, ("grp", DEV[2]), 0, 0, tiled=True).sum(axis=0)
    return emit + albedo * gathered


def solution(mesh):
    split = Mesh(
        mesh.devices.reshape(mesh.shape["grp"], 16, 4, 2), ("grp", "dev_0", "dev_1", "dev_2")
    )
    placed = (
        P(None, DEV),
        P(None, DEV),
        P(None, DEV),
        P(DEV),
        P(DEV),
        P(None, DEV),
        P(None, DEV),
        P("grp", DEV),
        P("grp", DEV),
        P("grp", DEV),
    )
    return jax.shard_map(body, mesh=split, in_specs=placed, out_specs=P(None, DEV), check_vma=False)
```

```python
import functools
import math

import jax
import jax.numpy as jnp
from jax import lax
from jax.experimental import pallas as pl
from jax.experimental.pallas import tpu as pltpu
from jax.sharding import Mesh
from jax.sharding import PartitionSpec as P

TILE = 128
DEV = ("dev_0", "dev_1", "dev_2")
RUN = 3
RUNS = 48
STEP = 8
PACK = 20
FIELDS = 9
SOURCE = 16
OFFSETS = 248
SHIFT = 1 << 13
CHUNK = 640
NT_DIMS = (((1,), (1,)), ((), ()))


def lane_rows(array):
    return [array[:, at : at + TILE] for at in range(0, array.shape[1], TILE)]


def terms(array, count):
    parts = []
    for _ in range(count):
        parts.append(array.astype(jnp.bfloat16).astype(jnp.float32))
        array = array - parts[-1]
    return parts


def pack_kernel(
    radiosity, area, parent, position, angles, receiver, source, count, pack_out, local_out
):
    leaf_count = area.shape[1]
    node_count = position.shape[1]
    cluster_count = node_count - leaf_count
    sines = jnp.sin(angles[...])
    cosines = jnp.cos(angles[...])
    cos_e = cosines[1:2, :]
    nodes = [position[a : a + 1, :] for a in range(3)]
    nodes += [cosines[0:1, :] * cos_e, sines[0:1, :] * cos_e, sines[1:2, :]]
    clusters = lax.broadcasted_iota(jnp.int32, (cluster_count, leaf_count), 0)
    onehot = (clusters == parent[...]).astype(jnp.bfloat16)
    leaf_area = area[...]
    values = jnp.concatenate(
        [leaf_area, radiosity[...] * leaf_area, jnp.zeros((4, leaf_count), jnp.float32)], axis=0
    )
    sums = lax.dot_general(
        jnp.concatenate(terms(values, 3), axis=0).astype(jnp.bfloat16),
        onehot,
        NT_DIMS,
        preferred_element_type=jnp.float32,
    )
    sums = sums[0:8, :] + sums[8:16, :] + sums[16:24, :]
    cluster_area = sums[0:1, :]
    cluster_radiosity = sums[1:4, :] / cluster_area
    scale = cluster_area * (-1.0 / math.pi)
    slots = receiver.shape[1]
    tiles = lax.broadcasted_iota(jnp.int32, (8, slots), 0)
    lanes = lax.broadcasted_iota(jnp.int32, (8, slots), 1)
    live = lanes < count[...]
    member = jnp.where((tiles == receiver[...]) & live, 1.0, 0.0)
    before = (
        lax.broadcasted_iota(jnp.int32, (slots, slots), 0)
        < lax.broadcasted_iota(jnp.int32, (slots, slots), 1)
    ).astype(jnp.bfloat16)
    place = jnp.dot(member.astype(jnp.bfloat16), before, preferred_element_type=jnp.float32)
    held = jnp.sum(member, axis=1, keepdims=True)
    runs = jnp.broadcast_to(jnp.floor((held + (RUN - 0.5)) * (1.0 / RUN)), (8, slots))
    first = jnp.zeros((8, slots), jnp.float32)
    for t in range(7):
        first = first + jnp.where(tiles > t, runs[t : t + 1, :], 0.0)
    run = jnp.floor((place + 0.5) * (1.0 / RUN))
    turn = place - run * RUN
    spot = jnp.sum(member * (first + run + turn * RUNS), axis=0, keepdims=True)
    alive = jnp.sum(member, axis=0, keepdims=True)
    spot = jnp.where(alive > 0.0, spot, -1.0).astype(jnp.int32)
    to_spot = (lax.broadcasted_iota(jnp.int32, (2 * slots, slots), 0) == spot).astype(jnp.bfloat16)
    entries = jnp.broadcast_to((source[...] + 1).astype(jnp.float32), (8, slots))
    entries = entries.astype(jnp.bfloat16)
    ordered = lax.dot_general(entries, to_spot, NT_DIMS, preferred_element_type=jnp.float32)
    offsets = jnp.sum(
        jnp.where(lanes == OFFSETS - TILE + tiles, first, 0.0), axis=0, keepdims=True
    )
    rows = []
    for half in range(cluster_count // TILE):
        cols = slice(half * TILE, half * TILE + TILE)
        at = slice(leaf_count + half * TILE, leaf_count + half * TILE + TILE)
        rows += [nodes[a][:, at] for a in range(3)]
        rows += [nodes[a][:, at] * scale[:, cols] for a in range(3, 6)]
        rows += [cluster_radiosity[c : c + 1, cols] for c in range(3)]
    rows += [ordered[0:1, :TILE], ordered[0:1, TILE:] + offsets]
    for piece in range(PACK // 4):
        part = jnp.concatenate(rows[piece * 4 : piece * 4 + 4], axis=0)
        pack_out[piece] = part
    local = [row for field in nodes for row in lane_rows(field)]
    local += lane_rows(parent[...].astype(jnp.float32))
    local += [jnp.zeros((1, TILE), jnp.float32)] * (local_out.shape[0] * 4 - len(local))
    for piece in range(len(local) // 4):
        local_out[piece] = jnp.concatenate(local[piece * 4 : piece * 4 + 4], axis=0)


def gather_kernel(
    where_ref,
    own_ref,
    other_ref,
    emit_ref,
    albedo_ref,
    out_ref,
    emit_out,
    albedo_out,
    sources,
    dense,
    receivers,
    totals,
    table_vmem,
    table,
    sem,
    *,
    sizes,
    node_count,
    leaf_count,
):
    shard_z, shard_y, shard_c = sizes
    shards = shard_z * shard_y * shard_c
    tiles = 2 * shards
    per_c = shard_y * shard_z
    per_peer = node_count // shards
    chunks = node_count // TILE
    blocks = (own_ref, other_ref)
    emit_out[...] = emit_ref[...]
    albedo_out[...] = albedo_ref[...]
    local = per_c * PACK
    here = where_ref[0]
    core = here & (shard_c - 1)

    def tile_of(shard):
        low = shard * per_peer // TILE
        high = (shard * per_peer + per_peer - 1) // TILE
        split = jnp.where(high > low, high * TILE - shard * per_peer, per_peer)
        late = split * 2 < per_peer
        return jnp.where(late, high, low), split, late

    tile, split, late = tile_of(here)
    partner = here ^ 1
    _, partner_split, partner_late = tile_of(partner)
    helps = partner_split < per_peer
    helped = jnp.where(partner_late, 0, partner_split)
    helped_count = jnp.where(partner_late, partner_split, per_peer - partner_split)

    def list_rows(at):
        return jnp.concatenate(
            [ref[pl.ds(at, per_c, stride=PACK), :] for ref in blocks], axis=0
        )

    low = list_rows(2 * FIELDS)
    high = list_rows(2 * FIELDS + 1)
    lane = lax.broadcasted_iota(jnp.int32, (shards, TILE), 1)
    arrival = lax.broadcasted_iota(jnp.int32, (shards, TILE), 0)
    first = jnp.sum(jnp.where(lane == OFFSETS - TILE + tile, high, 0.0), axis=1, keepdims=True)
    last = jnp.sum(jnp.where(lane == OFFSETS - TILE + tile + 1, high, 0.0), axis=1, keepdims=True)
    count = jnp.broadcast_to(last - first, (shards, TILE))
    upto = jnp.dot(
        (lane <= arrival).astype(jnp.bfloat16),
        count.astype(jnp.bfloat16),
        preferred_element_type=jnp.float32,
    )
    ahead = upto - count
    shift = first - ahead + SHIFT
    coarse = jnp.floor(shift * (1.0 / TILE))
    high = jnp.where(lane < OFFSETS - TILE, high, 0.0)
    extras = (arrival.astype(jnp.float32), coarse, shift - coarse * TILE, first)
    for n, extra in enumerate(extras):
        high = jnp.where(lane == OFFSETS - TILE + n, extra, high)
    listed = jnp.concatenate([low, high], axis=1).astype(jnp.bfloat16)

    def lay_out(chunk):
        spot = lax.broadcasted_iota(jnp.int32, (1, CHUNK), 1) + chunk * CHUNK
        place = spot.astype(jnp.float32)
        chosen = jnp.concatenate(
            [
                jnp.where((ahead <= part) & (part < upto), 1.0, 0.0)
                for part in lane_rows(place)
            ],
            axis=1,
        ).astype(jnp.bfloat16)
        found = lax.dot_general(
            listed, chosen, (((0,), (0,)), ((), ())), preferred_element_type=jnp.float32
        )
        owner = found[OFFSETS : OFFSETS + 1, :].astype(jnp.int32)
        run = found[OFFSETS + 1 : OFFSETS + 2, :] * TILE + found[OFFSETS + 2 : OFFSETS + 3, :]
        run = run - SHIFT + place
        goes_on = jnp.where(run > found[OFFSETS + 3 : OFFSETS + 4, :], 1, 0)
        runs = lax.broadcasted_iota(jnp.int32, (RUNS, CHUNK), 0).astype(jnp.float32)
        match = runs == run
        entries = jnp.concatenate(
            [
                jnp.sum(
                    jnp.where(match, found[u * RUNS : (u + 1) * RUNS, :], 0.0),
                    axis=0,
                    keepdims=True,
                )
                for u in range(RUN)
            ],
            axis=0,
        ).astype(jnp.int32)
        source = entries - 1
        giver = source >> 1
        came = (
            ((giver & (shard_c - 1)) ^ core) * per_c
            + ((giver >> (shard_c.bit_length() - 1)) & (shard_y - 1)) * shard_z
            + (giver >> ((shard_c * shard_y).bit_length() - 1))
        )
        rows = jnp.where(entries == 0, tiles, came * 2 + (source & 1)) * SOURCE
        link = (
            (owner & (shard_z - 1)) * (shard_y * shard_c)
            + ((owner >> (shard_z.bit_length() - 1)) & (shard_y - 1)) * shard_c
            + ((owner >> (per_c.bit_length() - 1)) ^ core)
        )
        total = jnp.concatenate([upto[shards - 1 : shards, :]] * (CHUNK // TILE), axis=1)
        total = total.astype(jnp.int32)
        link = jnp.where(spot < total, link, shards) * 8
        table_vmem[...] = jnp.concatenate(
            [rows, link, goes_on, total, jnp.zeros((5 - RUN, CHUNK), jnp.int32)], axis=0
        )
        return pltpu.make_async_copy(table_vmem, table, sem)

    fetch = lay_out(0)
    fetch.start()

    for c, ref in enumerate(blocks):
        for half in range(2):
            base = half * FIELDS
            rows = [ref[pl.ds(base + f, per_c, stride=PACK), :] for f in range(FIELDS)]
            length = jnp.sqrt(rows[3] * rows[3] + rows[4] * rows[4] + rows[5] * rows[5])
            rows += [length * math.pi, length]
            for f, row in enumerate(rows):
                at = c * per_c * 2 * SOURCE + half * SOURCE + f
                sources[pl.ds(at, per_c, stride=2 * SOURCE), :] = row
    blank = lax.broadcasted_iota(jnp.int32, (SOURCE, TILE), 0) >= FIELDS
    sources[tiles * SOURCE : (tiles + 1) * SOURCE, :] = blank.astype(jnp.float32)

    def spread(ref):
        for chunk in range(chunks):
            turned = ref[pl.ds(local + chunk, 8, stride=chunks), :].T
            for field in range(6):
                dense[field, 8 + chunk * TILE : 8 + (chunk + 1) * TILE, :] = jnp.broadcast_to(
                    turned[:, field : field + 1], (TILE, TILE)
                )

    for field in range(6):
        dense[field, 0:8, :] = jnp.zeros((8, TILE), jnp.float32)
        dense[field, 8 + node_count : 16 + node_count, :] = jnp.zeros((8, TILE), jnp.float32)
        receivers[field, shards * 8 : (shards + 8) * 8, :] = jnp.zeros((64, TILE), jnp.float32)
    spread(own_ref)

    def settle(link, carry):
        for field in range(6):
            receivers[field, pl.ds(pl.multiple_of(link * 8, 8), 8), :] = dense[
                field, pl.ds(8 + link * per_peer, 8), :
            ]
        return carry

    lax.fori_loop(0, shards, settle, 0, unroll=8)

    @pl.when(helps)
    def _():
        spread(other_ref)
        keep = lax.broadcasted_iota(jnp.int32, (8, TILE), 0) < per_peer

        def join(link, carry):
            for field in range(6):
                rows = pl.ds(pl.multiple_of(link * 8, 8), 8)
                theirs = dense[field, pl.ds(8 + link * per_peer + helped - per_peer, 8), :]
                receivers[field, rows, :] = jnp.where(keep, receivers[field, rows, :], theirs)
            return carry

        lax.fori_loop(0, shards, join, 0, unroll=4)

    for c in range(3):
        totals[c, :, :] = jnp.zeros(((shards + 8) * 8, TILE), jnp.float32)

    def step(turn, acc):
        for n in range(STEP):
            spot = turn * STEP + n
            at = pl.ds(pl.multiple_of(table[RUN, spot], 8), 8)
            keep = jnp.where(table[RUN + 1, spot] > 0, 1.0, 0.0)
            rec = [receivers[field, at, :] for field in range(6)]
            acc = [a * keep for a in acc]
            for u in range(RUN):
                row = pl.multiple_of(table[u, spot], SOURCE)
                src = [sources[pl.ds(row + f, 1), :] for f in range(FIELDS + 2)]
                d = [src[a] - rec[a] for a in range(3)]
                r2 = d[0] * d[0] + d[1] * d[1] + d[2] * d[2]
                toward = rec[3] * d[0] + rec[4] * d[1] + rec[5] * d[2]
                back = src[3] * d[0] + src[4] * d[1] + src[5] * d[2]
                top = jnp.maximum(toward, 0.0) * jnp.maximum(back, 0.0)
                factor = top / ((r2 + src[9]) * (r2 + src[10]))
                acc = [acc[c] + factor * src[6 + c] for c in range(3)]
            for c in range(3):
                totals[c, at, :] = acc[c]
        return acc

    def work_off(chunk, acc):
        held = jnp.clip(table[RUN + 2, 0] - chunk * CHUNK, 0, CHUNK)
        return lax.fori_loop(0, (held + STEP - 1) // STEP, step, acc)

    def next_chunk(chunk, acc):
        again = lay_out(chunk)
        again.start()
        again.wait()
        return work_off(chunk, acc)

    zero = jnp.zeros((8, TILE), jnp.float32)
    fetch.wait()
    acc = work_off(0, [zero] * 3)
    lax.fori_loop(1, (table[RUN + 2, 0] + CHUNK - 1) // CHUNK, next_chunk, acc)

    places = shards * 8
    band = lax.broadcasted_iota(jnp.int32, (TILE, TILE), 1)
    sums = jnp.zeros((places, TILE), jnp.float32)
    for c in range(3):
        to_band = (band == c).astype(jnp.bfloat16)
        whole = totals[c, 0:places, :]
        near = whole.astype(jnp.bfloat16)
        rest = (whole - near.astype(jnp.float32)).astype(jnp.bfloat16)
        for part in (near, rest):
            sums = sums + jnp.dot(part, to_band, preferred_element_type=jnp.float32)
    parts = jnp.concatenate(terms(sums.T[0:8, :], 2), axis=0).astype(jnp.bfloat16)
    place = lax.broadcasted_iota(jnp.int32, (places, TILE), 0)
    lane = lax.broadcasted_iota(jnp.int32, (places, TILE), 1)
    link = place >> 3
    slot = place & 7

    def collect(ref, node):
        pieces = []
        for chunk in range(leaf_count // TILE):
            parent = ref[pl.ds(local + 6 * chunks + chunk, 1), :].astype(jnp.int32) + leaf_count
            leaf = lane + chunk * TILE
            picked = jnp.where((node == leaf) | (node == parent), 1.0, 0.0)
            sums = jnp.dot(
                parts, picked.astype(jnp.bfloat16), preferred_element_type=jnp.float32
            )
            pieces.append(sums[0:3, :] + sums[8:11, :])
        return jnp.concatenate(pieces, axis=1)

    first_slot = jnp.where(late, split, 0)
    last_slot = jnp.where(late, per_peer, split)
    mine = (slot >= first_slot) & (slot < last_slot)
    result = collect(own_ref, jnp.where(mine, link * per_peer + slot, -1))
    groups = out_ref.shape[0] // shard_c
    for group in range(groups):
        out_ref[group * shard_c + core] = result

    @pl.when(helps)
    def _():
        theirs = (slot >= per_peer) & (slot < per_peer + helped_count)
        node = jnp.where(theirs, link * per_peer + helped + slot - per_peer, -1)
        result = collect(other_ref, node)
        for group in range(groups):
            out_ref[group * shard_c + 1 - core] = result

    @pl.when(jnp.logical_not(helps))
    def _():
        for group in range(groups):
            out_ref[group * shard_c + 1 - core] = jnp.zeros((3, leaf_count), jnp.float32)


def gather_call(where, own, other, emit, albedo, sizes, groups, node_count, leaf_count):
    shards = sizes[0] * sizes[1] * sizes[2]
    return pl.pallas_call(
        functools.partial(
            gather_kernel, sizes=sizes, node_count=node_count, leaf_count=leaf_count
        ),
        out_shape=(
            jax.ShapeDtypeStruct((groups * sizes[2], 3, leaf_count), jnp.float32),
            jax.ShapeDtypeStruct(emit.shape, jnp.float32),
            jax.ShapeDtypeStruct(albedo.shape, jnp.float32),
        ),
        in_specs=[pl.BlockSpec(memory_space=pltpu.SMEM)]
        + [pl.BlockSpec(memory_space=pltpu.VMEM)] * 4,
        out_specs=(pl.BlockSpec(memory_space=pltpu.VMEM),) * 3,
        scratch_shapes=[
            pltpu.VMEM(((2 * shards + 1) * SOURCE, TILE), jnp.float32),
            pltpu.VMEM((6, node_count + 16, TILE), jnp.float32),
            pltpu.VMEM((6, (shards + 8) * 8, TILE), jnp.float32),
            pltpu.VMEM((3, (shards + 8) * 8, TILE), jnp.float32),
            pltpu.VMEM((8, CHUNK), jnp.int32),
            pltpu.SMEM((8, CHUNK), jnp.int32),
            pltpu.SemaphoreType.DMA(()),
        ],
        compiler_params=pltpu.CompilerParams(vmem_limit_bytes=20 * 1024 * 1024),
        name="gather",
    )(where, own, other, emit, albedo)


def body(
    leaf_emit,
    leaf_albedo,
    leaf_radiosity,
    leaf_area,
    parent_index,
    node_position,
    node_angles,
    block_receiver,
    block_source,
    block_count,
):
    leaf_count = leaf_area.shape[0]
    node_count = node_position.shape[1]
    sizes = tuple(lax.axis_size(axis) for axis in DEV)
    groups = lax.axis_size("grp")
    vmem = pl.BlockSpec(memory_space=pltpu.VMEM)
    own_rows = 8 * node_count // TILE
    held, local = pl.pallas_call(
        pack_kernel,
        out_shape=(
            jax.ShapeDtypeStruct((PACK // 4, 4, TILE), jnp.float32),
            jax.ShapeDtypeStruct((own_rows // 4, 4, TILE), jnp.float32),
        ),
        in_specs=[vmem] * 8,
        out_specs=(vmem, vmem),
        name="pack",
    )(
        leaf_radiosity,
        leaf_area[None, :],
        parent_index[None, :],
        node_position,
        node_angles,
        block_receiver,
        block_source,
        block_count,
    )
    held = lax.all_to_all(
        jnp.broadcast_to(held[None], (sizes[0], *held.shape)), DEV[0], 0, 0, tiled=True
    ).reshape(-1, 4, TILE)
    held = lax.all_to_all(
        jnp.broadcast_to(held[None], (sizes[1], *held.shape)), DEV[1], 0, 0, tiled=True
    )
    held = jnp.concatenate([held.reshape(-1, 4, TILE), local], axis=0)
    other = lax.ppermute(held, DEV[2], [(0, 1), (1, 0)])
    where = lax.axis_index(DEV).astype(jnp.int32).reshape(1)
    partial, emit, albedo = gather_call(
        where,
        held.reshape(-1, TILE),
        other.reshape(-1, TILE),
        leaf_emit,
        leaf_albedo,
        sizes,
        groups,
        node_count,
        leaf_count,
    )
    gathered = lax.all_to_all(partial, ("grp", DEV[2]), 0, 0, tiled=True).sum(axis=0)
    return emit + albedo * gathered


def solution(mesh):
    split = Mesh(
        mesh.devices.reshape(mesh.shape["grp"], 16, 4, 2), ("grp", "dev_0", "dev_1", "dev_2")
    )
    placed = (
        P(None, DEV),
        P(None, DEV),
        P(None, DEV),
        P(DEV),
        P(DEV),
        P(None, DEV),
        P(None, DEV),
        P("grp", DEV),
        P("grp", DEV),
        P("grp", DEV),
    )
    return jax.shard_map(body, mesh=split, in_specs=placed, out_specs=P(None, DEV), check_vma=False)
```
